256 devices in a mesh: ctx: 32 (over z, y), dp: 8 (over x, core).
Axes of the slice: x: 4, y: 4, z: 8, core: 2. Of those that a mesh axis runs over, the one named last changes fastest.
Arguments:
- queries: bfloat16 [24576, 8192], P('ctx', 'dp'), may hold values from -96 to 96
- keys: bfloat16 [24576, 1024], P(('ctx', 'dp')), may hold values from -36 to 36
- values: bfloat16 [24576, 1024], P(('ctx', 'dp')), may hold values from -6 to 6
- grad_out: bfloat16 [24576, 8192], P('ctx', 'dp'), may hold values from -6 to 6
- doc_lengths: int32 [64], replicated, may hold values from 1 to 768, 24576 in all
Outputs:
- attn_out: bfloat16 [24576, 8192], P('ctx', 'dp')
- grad_q: bfloat16 [24576, 8192], P('ctx', 'dp')
- grad_k: bfloat16 [24576, 1024], P(('ctx', 'dp'))
- grad_v: bfloat16 [24576, 1024], P(('ctx', 'dp'))
The draws below stay inside these ranges and needn't reach their ends.
Inputs may be any that keep to these rules, and one draw needn't show every extreme that they name: `doc_lengths`: the lengths sum to 24576.
All inputs are finite; a program needn't handle non-finite values.
Results may differ from the reference program's by a relative error of at most 0.02.
Values may be sent and summed in bfloat16 or wider, within the bound.
No kernel may reach another device: no remote copies, remote signals or barrier semaphores. Data moves between devices by JAX's collectives and lax.ppermute only.
A program may use at most 64 MiB of HBM per device.

```python
import math
import jax
import jax.numpy as jnp
import numpy as np
from jax import lax

HEADS = 64
KVH = 8
HD = 128
T_DEV = 768
TOKENS = 24576
MOST_DOC = 768
NDOCS = 64
N_CTX = 32


def draw_queries(key, part):
    normal_draw = jnp.clip(jax.random.normal(key, (TOKENS, HEADS, HD), jnp.float32), -6.0, 6.0)
    return normal_draw.reshape(TOKENS, HEADS * HD).astype(jnp.bfloat16)


def draw_keys(key, part):
    normal_draw = jnp.clip(jax.random.normal(key, (TOKENS, KVH * HD), jnp.float32), -6.0, 6.0)
    return normal_draw.astype(jnp.bfloat16)


def steps_of(rng, extent, pieces, least, top_value):
    factor_of = 1.0
    for axis_at, shards_of in pieces:
        steps = jax.random.uniform(jax.random.fold_in(jax.random.fold_in(rng, 6), axis_at), (shards_of,), jnp.float32, least / len(pieces), top_value / len(pieces))
        factor_of = factor_of * jnp.repeat(jnp.exp(steps), extent[axis_at] // shards_of).reshape((-1,) + (1,) * (len(extent) - 1 - axis_at))
    return factor_of


def split_up(amount, total, reach, skew):
    loads = [(1 << 20) // math.isqrt(rank ** skew) + 1 for rank in range(2, amount + 1)]
    surplus, given = total - reach - (amount - 1), [1] * (amount - 1)
    while surplus > 0:
        movable = [i for i in range(amount - 1) if given[i] < reach]
        pool, left = sum([loads[i] for i in movable]), surplus
        for i in movable:
            addition = min(reach - given[i], max(1, left * loads[i] // pool), surplus)
            given[i] = given[i] + addition
            surplus = surplus - addition
    return np.array([reach] + given)


def uneven(own_key, count, total, limit, skew):
    if count == 2:
        one = jax.random.randint(own_key, (), max(1, total - limit), min(limit, total - 1) + 1)
        return jnp.stack([one, total - one])
    lengths = jnp.asarray(split_up(count, total, limit, skew), jnp.int32)
    twos = (count - 1) // 2
    source_of, sink = lengths[1:1 + 2 * twos:2], lengths[2:2 + 2 * twos:2]
    slack = jnp.minimum(source_of - 1, limit - sink)
    passed = jax.random.randint(jax.random.fold_in(own_key, 1), (twos,), 0, 1 << 20) % (slack + 1)
    lengths = lengths.at[1:1 + 2 * twos:2].set(source_of - passed).at[2:2 + 2 * twos:2].set(sink + passed)
    return lengths[jax.random.permutation(jax.random.fold_in(own_key, 2), count)]


def scatter_about(own_key, dims, scale, reach, shards=(), kind=jnp.bfloat16):
    entries = scale * jax.random.normal(own_key, dims, jnp.float32)
    if shards:
        entries = entries * steps_of(own_key, dims, shards, -0.22, 0.18)
    return jnp.clip(entries, -reach, reach).astype(kind)


def setup_inputs(seed: int = 0) -> dict:
    seeds = jax.random.split(jax.random.key(seed), 6)
    queries = draw_queries(jax.random.fold_in(seeds[5], 71), 0)
    keys = draw_keys(jax.random.fold_in(seeds[5], 71), 0)
    values = scatter_about(seeds[2], (TOKENS, KVH * HD), 1.0, 6.0, ((0, 256),))
    grad_out = scatter_about(seeds[3], (TOKENS, HEADS * HD), 1.0, 6.0, ((0, 32), (1, 8)))
    doc_lengths = uneven(seeds[4], NDOCS, TOKENS, MOST_DOC, 2).astype(jnp.int32)
    return {"queries": queries, "keys": keys, "values": values, "grad_out": grad_out, "doc_lengths": doc_lengths}


NEGATIVE = -1e+30

def doc_index(positions, doc_ends):
    return lax.optimization_barrier(jnp.sum((doc_ends[None, :] <= positions[:, None]).astype(jnp.int32), axis=1))

def reference(queries, keys, values, grad_out, doc_lengths):
    score_scale = 1.0 / math.sqrt(HD)
    doc_ends = jnp.cumsum(doc_lengths).astype(jnp.int32)
    window = 2 * T_DEV
    margin = T_DEV
    per_group = HEADS // KVH
    padding = jnp.zeros((margin, KVH * HD), jnp.bfloat16)
    keys_padded = jnp.concatenate([padding, keys], axis=0)
    values_padded = jnp.concatenate([padding, values], axis=0)

    def one_block(block_idx):
        start_row = (block_idx * T_DEV).astype(jnp.int32)
        query_block = lax.dynamic_slice_in_dim(queries, start_row, T_DEV, 0).astype(jnp.float32).reshape(T_DEV, KVH, per_group, HD)
        grad_block = lax.dynamic_slice_in_dim(grad_out, start_row, T_DEV, 0).astype(jnp.float32).reshape(T_DEV, KVH, per_group, HD)
        key_block = lax.dynamic_slice_in_dim(keys_padded, start_row, window, 0).astype(jnp.float32).reshape(window, KVH, HD)
        value_block = lax.dynamic_slice_in_dim(values_padded, start_row, window, 0).astype(jnp.float32).reshape(window, KVH, HD)
        query_pos = start_row + jnp.arange(T_DEV, dtype=jnp.int32)
        key_pos = start_row - margin + jnp.arange(window, dtype=jnp.int32)
        allowed = (doc_index(query_pos, doc_ends)[:, None] == doc_index(key_pos, doc_ends)[None, :]) & (key_pos[None, :] <= query_pos[:, None]) & (key_pos[None, :] >= 0)
        scores = jnp.einsum('tgjd,sgd->gjts', query_block, key_block) * score_scale
        scores = jnp.where(allowed[None, None], scores, NEGATIVE)
        row_max = lax.optimization_barrier(jnp.max(scores, axis=-1, keepdims=True))
        log_total = row_max + jnp.log(lax.optimization_barrier(jnp.sum(jnp.exp(scores - row_max), axis=-1, keepdims=True)))
        weights_full = jnp.exp(scores - log_total)
        weights = weights_full.astype(jnp.bfloat16).astype(jnp.float32)
        output = jnp.einsum('gjts,sgd->tgjd', weights, value_block).astype(jnp.bfloat16)
        row_delta = lax.optimization_barrier(jnp.sum(grad_block * output.astype(jnp.float32), axis=-1))
        grad_weights = jnp.einsum('tgjd,sgd->gjts', grad_block, value_block)
        grad_scores = (weights_full * (grad_weights - jnp.transpose(row_delta, (1, 2, 0))[..., None])).astype(jnp.bfloat16).astype(jnp.float32)
        grad_query = (jnp.einsum('gjts,sgd->tgjd', grad_scores, key_block) * score_scale).astype(jnp.bfloat16)
        grad_key = jnp.einsum('gjts,tgjd->sgd', grad_scores, query_block) * score_scale
        grad_value = jnp.einsum('gjts,tgjd->sgd', weights, grad_block)
        return (output.reshape(T_DEV, HEADS * HD), grad_query.reshape(T_DEV, HEADS * HD), grad_key.reshape(window, KVH * HD), grad_value.reshape(window, KVH * HD))
    outputs, grads_query, key_parts, value_parts = lax.map(one_block, jnp.arange(N_CTX, dtype=jnp.int32))

    def add_block(block_idx, totals):
        key_total, value_total = totals
        start_row = (block_idx * T_DEV).astype(jnp.int32)
        key_total = lax.dynamic_update_slice_in_dim(key_total, lax.dynamic_slice_in_dim(key_total, start_row, window, 0) + key_parts[block_idx], start_row, 0)
        value_total = lax.dynamic_update_slice_in_dim(value_total, lax.dynamic_slice_in_dim(value_total, start_row, window, 0) + value_parts[block_idx], start_row, 0)
        return (key_total, value_total)
    zero_rows = jnp.zeros((margin + TOKENS, KVH * HD), jnp.float32)
    key_total, value_total = lax.fori_loop(0, N_CTX, add_block, (zero_rows, zero_rows))
    attn_out = outputs.reshape(TOKENS, HEADS * HD)
    grad_q = grads_query.reshape(TOKENS, HEADS * HD)
    return (attn_out, grad_q, key_total[margin:].astype(jnp.bfloat16), value_total[margin:].astype(jnp.bfloat16))
```

```python
import functools, math
import jax, jax.numpy as jnp
from jax import lax
from jax.experimental import pallas as pl
from jax.experimental.pallas import tpu as pltpu
from jax.sharding import PartitionSpec as P

HD = 128
TILE = 128
NEG = -1e30
F32 = jnp.float32
BF16 = jnp.bfloat16


def dot_nt(a, b):
    return lax.dot_general(a, b, (((1,), (1,)), ((), ())), preferred_element_type=F32)


def dot_tn(a, b):
    return lax.dot_general(a, b, (((0,), (0,)), ((), ())), preferred_element_type=F32)


def dot_nn(a, b):
    return lax.dot_general(a, b, (((1,), (0,)), ((), ())), preferred_element_type=F32)


def kernel(G, unroll, form, n_ref, start_ref, q_ref, g_ref, kvp_ref, kvo_ref, out_ref, dq_ref, dkvp_ref, dkvo_ref,
           k_s, v_s, bias_s, dk_s, dv_s):
    i = pl.program_id(0)
    tiles = pl.num_programs(0)
    rows = kvp_ref.shape[0]
    heads = q_ref.shape[1] // HD
    scale = 1.0 / math.sqrt(HD)
    c = scale * math.log2(math.e)

    @pl.when(i == 0)
    def _():
        k_s[:rows, :] = kvp_ref[:, :HD]
        k_s[rows:, :] = kvo_ref[:, :HD]
        v_s[:rows, :HD] = kvp_ref[:, HD:]
        v_s[rows:, :HD] = kvo_ref[:, HD:]
        v_s[:, HD:] = jnp.ones((2 * rows, HD), BF16)
        dk_s[...] = jnp.zeros_like(dk_s)
        dv_s[...] = jnp.zeros_like(dv_s)

    n = n_ref[i]
    last = i + rows // TILE
    startc = jnp.transpose(jnp.broadcast_to(start_ref[0], (TILE, TILE)))
    lane = lax.broadcasted_iota(jnp.int32, (TILE, TILE), 1)
    row = lax.broadcasted_iota(jnp.int32, (TILE, TILE), 0)

    for w in range(1, rows // TILE + 2):
        @pl.when(n == w)
        def _(w=w):
            first = last - (w - 1)
            for j in range(w):
                keep = (first + j) * TILE + lane >= startc
                if j == w - 1:
                    keep = keep & (lane <= row)
                bias_s[:, j * TILE:(j + 1) * TILE] = jnp.where(keep, 0.0, NEG)
            keys = pl.ds(pl.multiple_of(first * TILE, TILE), w * TILE)

            def group(hg, carry):
                k = k_s[keys, :]
                v1 = v_s[keys, :]
                bias = bias_s[:, :w * TILE]
                cols = [pl.ds(pl.multiple_of((hg * G + a) * HD, HD), HD) for a in range(G)]
                q = jnp.concatenate([q_ref[:, col] for col in cols], axis=0)
                g = jnp.concatenate([g_ref[:, col] for col in cols], axis=0)
                t = dot_nt(q, k) * c
                t = (t.reshape(G, TILE, w * TILE) + bias[None]).reshape(G * TILE, w * TILE)
                m = jnp.max(t, axis=1, keepdims=True)
                p = jnp.exp2(t - m)
                pb = p.astype(BF16)
                o1 = dot_nn(pb, v1)
                inv = 1.0 / o1[:, HD:]
                out = (o1[:, :HD] * inv).astype(BF16)
                gs = (g.astype(F32) * inv).astype(BF16)
                delta = jnp.sum(gs.astype(F32) * out.astype(F32), axis=1, keepdims=True)
                dp = dot_nt(gs, v1[:, :HD])
                ds = (p * (dp - delta)).astype(BF16)
                dq = (dot_nn(ds, k) * scale).astype(BF16)
                for a, col in enumerate(cols):
                    out_ref[:, col] = out[a * TILE:(a + 1) * TILE]
                    dq_ref[:, col] = dq[a * TILE:(a + 1) * TILE]
                if form == "tn":
                    dk_s[keys, :] += dot_tn(ds, q)
                    dv_s[keys, :] += dot_tn(pb, gs)
                else:
                    dk = dot_nn(jnp.transpose(q), ds)
                    dv = dot_nn(jnp.transpose(gs), pb)
                    for j in range(w):
                        at = pl.ds(pl.multiple_of((first + j) * TILE, TILE), TILE)
                        dk_s[at, :] += dk[:, j * TILE:(j + 1) * TILE]
                        dv_s[at, :] += dv[:, j * TILE:(j + 1) * TILE]
                return carry

            lax.fori_loop(0, heads // G, group, 0, unroll=unroll)

    @pl.when(i == tiles - 1)
    def _():
        for j in range(2 * rows // TILE):
            sl = slice(j * TILE, (j + 1) * TILE)
            dk, dv = dk_s[sl, :], dv_s[sl, :]
            if form != "tn":
                dk, dv = jnp.transpose(dk), jnp.transpose(dv)
            dk = dk * scale
            ref = dkvp_ref if j < rows // TILE else dkvo_ref
            o = j * TILE % rows
            ref[o:o + TILE, :HD] = dk.astype(ref.dtype)
            ref[o:o + TILE, HD:] = dv.astype(ref.dtype)


def attention(n_tiles, starts, q, g, kvp, kvo, G=2, unroll=1, form="tn"):
    rows = q.shape[0]
    tiles = rows // TILE
    width = q.shape[1]
    whole = lambda i, *_: (0, 0)
    tile = lambda i, *_: (i, 0)
    return pl.pallas_call(
        functools.partial(kernel, G, unroll, form),
        grid_spec=pltpu.PrefetchScalarGridSpec(
            num_scalar_prefetch=1, grid=(tiles,),
            in_specs=[
                pl.BlockSpec((1, 1, TILE), lambda i, *_: (i, 0, 0)),
                pl.BlockSpec((TILE, width), tile),
                pl.BlockSpec((TILE, width), tile),
                pl.BlockSpec((rows, 2 * HD), whole),
                pl.BlockSpec((rows, 2 * HD), whole),
            ],
            out_specs=[
                pl.BlockSpec((TILE, width), tile),
                pl.BlockSpec((TILE, width), tile),
                pl.BlockSpec((rows, 2 * HD), whole),
                pl.BlockSpec((rows, 2 * HD), whole),
            ],
            scratch_shapes=[
                pltpu.VMEM((2 * rows, HD), BF16),
                pltpu.VMEM((2 * rows, 2 * HD), BF16),
                pltpu.VMEM((TILE, rows + TILE), F32),
                pltpu.VMEM((2 * rows, HD), F32),
                pltpu.VMEM((2 * rows, HD), F32),
            ]),
        out_shape=[
            jax.ShapeDtypeStruct(q.shape, BF16),
            jax.ShapeDtypeStruct(q.shape, BF16),
            jax.ShapeDtypeStruct((rows, 2 * HD), BF16),
            jax.ShapeDtypeStruct((rows, 2 * HD), F32),
        ],
        compiler_params=pltpu.CompilerParams(dimension_semantics=("arbitrary",), vmem_limit_bytes=48 << 20),
        name="masked_attention",
    )(n_tiles, starts, q, g, kvp, kvo)


def passed_along(x, axis, by):
    count = lax.axis_size(axis)
    pairs = [(i, i + by) for i in range(count) if 0 <= i + by < count]
    return lax.ppermute(x, axis, pairs)


def by_head(x):
    return jnp.transpose(x.reshape(x.shape[0], -1, HD), (1, 0, 2))


def by_token(x):
    return jnp.transpose(x, (1, 0, 2)).reshape(x.shape[1], -1)


def per_device(queries, keys, values, grad_out, doc_lengths):
    rows = queries.shape[0]
    shared = jnp.concatenate([by_head(keys), by_head(values)], axis=2)
    own = lax.all_to_all(shared, "dp", split_axis=0, concat_axis=0, tiled=True).reshape(rows, 2 * HD)
    prev = passed_along(own, "ctx", 1)
    first_pos = lax.axis_index("ctx") * rows
    ends = jnp.cumsum(doc_lengths)
    positions = first_pos + jnp.arange(rows, dtype=jnp.int32)
    starts = jnp.max(jnp.where(ends[None, :] <= positions[:, None], ends[None, :], 0), axis=1)
    starts = (starts - first_pos + rows).astype(jnp.int32)
    tiles = rows // TILE
    last = jnp.arange(tiles, dtype=jnp.int32) + tiles
    n_tiles = last - starts[::TILE] // TILE + 1
    attn_out, grad_q, back, mine = attention(
        n_tiles, starts.reshape(tiles, 1, TILE), queries, grad_out, prev, own, form="nn"
    )
    total = (mine + passed_along(back, "ctx", -1).astype(F32)).astype(BF16)
    total = total.reshape(shared.shape)
    grads = lax.all_to_all(total, "dp", split_axis=0, concat_axis=0, tiled=True)
    return attn_out, grad_q, by_token(grads[:, :, :HD]), by_token(grads[:, :, HD:])


def solution(mesh):
    placed = (P("ctx", "dp"), P(("ctx", "dp"), None), P(("ctx", "dp"), None), P("ctx", "dp"), P())
    return jax.shard_map(
        per_device,
        mesh=mesh,
        in_specs=placed,
        out_specs=(P("ctx", "dp"), P("ctx", "dp"), P(("ctx", "dp"), None), P(("ctx", "dp"), None)),
        check_vma=False,
    )
```

```python
import functools, math
import jax, jax.numpy as jnp
from jax import lax
from jax.experimental import pallas as pl
from jax.experimental.pallas import tpu as pltpu
from jax.sharding import PartitionSpec as P

HD = 128
TILE = 128
NEG = -1e30
F32 = jnp.float32
BF16 = jnp.bfloat16


def dot_nt(a, b):
    return lax.dot_general(a, b, (((1,), (1,)), ((), ())), preferred_element_type=F32)


def dot_tn(a, b):
    return lax.dot_general(a, b, (((0,), (0,)), ((), ())), preferred_element_type=F32)


def dot_nn(a, b):
    return lax.dot_general(a, b, (((1,), (0,)), ((), ())), preferred_element_type=F32)


def kernel(G, unroll, form, n_ref, start_ref, q_ref, g_ref, kvp_ref, kvo_ref, out_ref, dq_ref, dkvp_ref, dkvo_ref,
           k_s, v_s, bias_s, dk_s, dv_s):
    i = pl.program_id(0)
    tiles = pl.num_programs(0)
    rows = kvp_ref.shape[0]
    heads = q_ref.shape[1] // HD
    scale = 1.0 / math.sqrt(HD)
    c = scale * math.log2(math.e)

    @pl.when(i == 0)
    def _():
        k_s[:rows, :] = kvp_ref[:, :HD]
        k_s[rows:, :] = kvo_ref[:, :HD]
        v_s[:rows, :HD] = kvp_ref[:, HD:]
        v_s[rows:, :HD] = kvo_ref[:, HD:]
        v_s[:, HD:] = jnp.ones((2 * rows, HD), BF16)
        dk_s[...] = jnp.zeros_like(dk_s)
        dv_s[...] = jnp.zeros_like(dv_s)

    n = n_ref[i]
    last = i + rows // TILE
    startc = jnp.transpose(jnp.broadcast_to(start_ref[0], (TILE, TILE)))
    lane = lax.broadcasted_iota(jnp.int32, (TILE, TILE), 1)
    row = lax.broadcasted_iota(jnp.int32, (TILE, TILE), 0)

    for w in range(1, rows // TILE + 2):
        @pl.when(n == w)
        def _(w=w):
            first = last - (w - 1)
            for j in range(w):
                keep = (first + j) * TILE + lane >= startc
                if j == w - 1:
                    keep = keep & (lane <= row)
                bias_s[:, j * TILE:(j + 1) * TILE] = jnp.where(keep, 0.0, NEG)
            keys = pl.ds(pl.multiple_of(first * TILE, TILE), w * TILE)

            def group(hg, carry):
                k = k_s[keys, :]
                v1 = v_s[keys, :]
                bias = bias_s[:, :w * TILE]
                cols = [pl.ds(pl.multiple_of((hg * G + a) * HD, HD), HD) for a in range(G)]
                q = jnp.concatenate([q_ref[:, col] for col in cols], axis=0)
                g = jnp.concatenate([g_ref[:, col] for col in cols], axis=0)
                t = dot_nt(q, k) * c
                t = (t.reshape(G, TILE, w * TILE) + bias[None]).reshape(G * TILE, w * TILE)
                m = jnp.max(t, axis=1, keepdims=True)
                p = jnp.exp2(t - m)
                pb = p.astype(BF16)
                o1 = dot_nn(pb, v1)
                inv = 1.0 / o1[:, HD:]
                out = (o1[:, :HD] * inv).astype(BF16)
                gs = (g.astype(F32) * inv).astype(BF16)
                delta = jnp.sum(gs.astype(F32) * out.astype(F32), axis=1, keepdims=True)
                dp = dot_nt(gs, v1[:, :HD])
                ds = (p * (dp - delta)).astype(BF16)
                dq = (dot_nn(ds, k) * scale).astype(BF16)
                for a, col in enumerate(cols):
                    out_ref[:, col] = out[a * TILE:(a + 1) * TILE]
                    dq_ref[:, col] = dq[a * TILE:(a + 1) * TILE]
                if form == "tn":
                    dk_s[keys, :] += dot_tn(ds, q)
                    dv_s[keys, :] += dot_tn(pb, gs)
                else:
                    dk = dot_nn(jnp.transpose(q), ds)
                    dv = dot_nn(jnp.transpose(gs), pb)
                    for j in range(w):
                        at = pl.ds(pl.multiple_of((first + j) * TILE, TILE), TILE)
                        dk_s[at, :] += dk[:, j * TILE:(j + 1) * TILE]
                        dv_s[at, :] += dv[:, j * TILE:(j + 1) * TILE]
                return carry

            lax.fori_loop(0, heads // G, group, 0, unroll=unroll)

    @pl.when(i == tiles - 1)
    def _():
        for j in range(2 * rows // TILE):
            sl = slice(j * TILE, (j + 1) * TILE)
            dk, dv = dk_s[sl, :], dv_s[sl, :]
            if form != "tn":
                dk, dv = jnp.transpose(dk), jnp.transpose(dv)
            dk = dk * scale
            ref = dkvp_ref if j < rows // TILE else dkvo_ref
            o = j * TILE % rows
            ref[o:o + TILE, :HD] = dk.astype(ref.dtype)
            ref[o:o + TILE, HD:] = dv.astype(ref.dtype)


def attention(n_tiles, starts, q, g, kvp, kvo, G=2, unroll=1, form="tn"):
    rows = q.shape[0]
    tiles = rows // TILE
    width = q.shape[1]
    whole = lambda i, *_: (0, 0)
    tile = lambda i, *_: (i, 0)
    return pl.pallas_call(
        functools.partial(kernel, G, unroll, form),
        grid_spec=pltpu.PrefetchScalarGridSpec(
            num_scalar_prefetch=1, grid=(tiles,),
            in_specs=[
                pl.BlockSpec((1, 1, TILE), lambda i, *_: (i, 0, 0)),
                pl.BlockSpec((TILE, width), tile),
                pl.BlockSpec((TILE, width), tile),
                pl.BlockSpec((rows, 2 * HD), whole),
                pl.BlockSpec((rows, 2 * HD), whole),
            ],
            out_specs=[
                pl.BlockSpec((TILE, width), tile),
                pl.BlockSpec((TILE, width), tile),
                pl.BlockSpec((rows, 2 * HD), whole),
                pl.BlockSpec((rows, 2 * HD), whole),
            ],
            scratch_shapes=[
                pltpu.VMEM((2 * rows, HD), BF16),
                pltpu.VMEM((2 * rows, 2 * HD), BF16),
                pltpu.VMEM((TILE, rows + TILE), F32),
                pltpu.VMEM((2 * rows, HD), F32),
                pltpu.VMEM((2 * rows, HD), F32),
            ]),
        out_shape=[
            jax.ShapeDtypeStruct(q.shape, BF16),
            jax.ShapeDtypeStruct(q.shape, BF16),
            jax.ShapeDtypeStruct((rows, 2 * HD), BF16),
            jax.ShapeDtypeStruct((rows, 2 * HD), F32),
        ],
        compiler_params=pltpu.CompilerParams(dimension_semantics=("arbitrary",), vmem_limit_bytes=48 << 20),
        name="masked_attention",
    )(n_tiles, starts, q, g, kvp, kvo)


def passed_along(x, axis, by):
    count = lax.axis_size(axis)
    pairs = [(i, i + by) for i in range(count) if 0 <= i + by < count]
    return lax.ppermute(x, axis, pairs)


def by_head(x):
    return jnp.transpose(x.reshape(x.shape[0], -1, HD), (1, 0, 2))


def by_token(x):
    return jnp.transpose(x, (1, 0, 2)).reshape(x.shape[1], -1)


def per_device(queries, keys, values, grad_out, doc_lengths):
    rows = queries.shape[0]
    shared = jnp.concatenate([by_head(keys), by_head(values)], axis=2)
    own = lax.all_to_all(shared, "dp", split_axis=0, concat_axis=0, tiled=True).reshape(rows, 2 * HD)
    prev = passed_along(own, "ctx", 1)
    first_pos = lax.axis_index("ctx") * rows
    ends = jnp.cumsum(doc_lengths)
    positions = first_pos + jnp.arange(rows, dtype=jnp.int32)
    starts = jnp.max(jnp.where(ends[None, :] <= positions[:, None], ends[None, :], 0), axis=1)
    starts = (starts - first_pos + rows).astype(jnp.int32)
    tiles = rows // TILE
    last = jnp.arange(tiles, dtype=jnp.int32) + tiles
    n_tiles = last - starts[::TILE] // TILE + 1
    attn_out, grad_q, back, mine = attention(
        n_tiles, starts.reshape(tiles, 1, TILE), queries, grad_out, prev, own, G=8, form="nn"
    )
    total = (mine + passed_along(back, "ctx", -1).astype(F32)).astype(BF16)
    total = total.reshape(shared.shape)
    grads = lax.all_to_all(total, "dp", split_axis=0, concat_axis=0, tiled=True)
    return attn_out, grad_q, by_token(grads[:, :, :HD]), by_token(grads[:, :, HD:])


def solution(mesh):
    placed = (P("ctx", "dp"), P(("ctx", "dp"), None), P(("ctx", "dp"), None), P("ctx", "dp"), P())
    return jax.shard_map(
        per_device,
        mesh=mesh,
        in_specs=placed,
        out_specs=(P("ctx", "dp"), P("ctx", "dp"), P(("ctx", "dp"), None), P(("ctx", "dp"), None)),
        check_vma=False,
    )
```

```python
import functools
import math

import jax
import jax.numpy as jnp
from jax import lax
from jax.experimental import pallas as pl
from jax.experimental.pallas import tpu as pltpu
from jax.sharding import PartitionSpec as P

HD = 128
TILE = 128
NEG = -1e30
F32 = jnp.float32
BF16 = jnp.bfloat16
SCALE = 1.0 / math.sqrt(HD)
LOG2_SCALE = SCALE * math.log2(math.e)


def dot_nt(a, b):
    return lax.dot_general(a, b, (((1,), (1,)), ((), ())), preferred_element_type=F32)


def dot_nn(a, b):
    return lax.dot_general(a, b, (((1,), (0,)), ((), ())), preferred_element_type=F32)


def by_rows(ref):
    return jnp.concatenate([ref[:, h * HD:(h + 1) * HD] for h in range(ref.shape[1] // HD)], axis=0)


def put_rows(ref, x):
    for h in range(ref.shape[1] // HD):
        ref[:, h * HD:(h + 1) * HD] = x[h * TILE:(h + 1) * TILE].astype(ref.dtype)


def write_bias(bias_ref, start_ref, first, count, offset, causal):
    startc = jnp.transpose(jnp.broadcast_to(start_ref[0], (TILE, TILE)))
    lane = lax.broadcasted_iota(jnp.int32, (TILE, TILE), 1)
    row = lax.broadcasted_iota(jnp.int32, (TILE, TILE), 0)
    for j in range(count):
        keep = lane >= startc - ((first + j) * TILE + offset)
        if causal and j == count - 1:
            keep = keep & (lane <= row)
        bias_ref[:, j * TILE:(j + 1) * TILE] = jnp.where(keep, 0.0, NEG)


def biased_scores(q, k, bias, heads):
    t = dot_nt(q, k) * LOG2_SCALE
    rows, width = t.shape
    return (t.reshape(heads, TILE, width) + bias[None]).reshape(rows, width)


def put_scaled(out_ref, gs_ref, out, gs):
    put_rows(out_ref, out)
    put_rows(gs_ref, gs)


def local_forward(n_ref, start_ref, q_ref, g_ref, kv_ref, p_ref, o_ref, max_ref, out_ref, gs_ref, v_s, bias_s):
    i = pl.program_id(0)
    tiles = pl.num_programs(0)
    rows = kv_ref.shape[0]
    heads = q_ref.shape[1] // HD

    @pl.when(i == 0)
    def _():
        v_s[:, :HD] = kv_ref[:, HD:]
        v_s[:, HD:] = jnp.ones((rows, HD), BF16)

    for w in range(1, rows // TILE + 1):
        @pl.when(n_ref[i] == w)
        def _(w=w):
            first = i - (w - 1)
            write_bias(bias_s, start_ref, first, w, rows, True)
            keys = pl.ds(pl.multiple_of(first * TILE, TILE), w * TILE)
            t = biased_scores(by_rows(q_ref), kv_ref[keys, :HD], bias_s[:, :w * TILE], heads)
            m = jnp.max(t, axis=1, keepdims=True)
            p = jnp.exp2(t - m).astype(BF16)
            p_ref[0, :, :w * TILE] = p
            o_ref[0] = dot_nn(p, v_s[keys, :])
            max_ref[0] = jnp.broadcast_to(m, max_ref.shape[1:])

    @pl.when(n_ref[tiles + i] == 0)
    def _():
        inv = 1.0 / o_ref[0, :, HD:]
        put_rows(out_ref, o_ref[0, :, :HD] * inv)
        put_rows(gs_ref, by_rows(g_ref).astype(F32) * inv)


def prev_step(n_ref, start_ref, q_ref, g_ref, kv_ref, o_ref, max_ref, out_in_ref, gs_in_ref,
              out_ref, gs_ref, dq_ref, dkv_ref, v_s, bias_s, dk_s, dv_s):
    i = pl.program_id(0)
    tiles = pl.num_programs(0)
    rows = kv_ref.shape[0]
    heads = q_ref.shape[1] // HD
    crossing = n_ref[2 * tiles]

    @pl.when(i == 0)
    def _():
        v_s[:, :HD] = kv_ref[:, HD:]
        v_s[:, HD:] = jnp.ones((rows, HD), BF16)
        dk_s[...] = jnp.zeros_like(dk_s)
        dv_s[...] = jnp.zeros_like(dv_s)

    @pl.when((i == 0) & (crossing == 0))
    def _():
        out_ref[...] = out_in_ref[...]
        gs_ref[...] = gs_in_ref[...]
        dq_ref[...] = jnp.zeros_like(dq_ref)

    for w in range(1, rows // TILE + 1):
        @pl.when(n_ref[tiles + i] == w)
        def _(w=w):
            first = rows // TILE - w
            write_bias(bias_s, start_ref, first, w, 0, False)
            keys = slice(first * TILE, rows)
            q = by_rows(q_ref)
            g = by_rows(g_ref).astype(F32)
            k = kv_ref[keys, :HD]
            t = biased_scores(q, k, bias_s[:, :w * TILE], heads)
            m1 = max_ref[0]
            m = jnp.maximum(m1, jnp.max(t, axis=1, keepdims=True))
            a1 = jnp.exp2(m1 - m)
            p = jnp.exp2(t - jnp.concatenate([m] * w, axis=1))
            pb = p.astype(BF16)
            o2 = dot_nn(pb, v_s[keys, :])
            inv = 1.0 / (a1 * o_ref[0, :, HD:] + o2[:, HD:])
            out = ((a1 * o_ref[0, :, :HD] + o2[:, :HD]) * inv).astype(BF16)
            g = g * inv
            gs = g.astype(BF16)
            put_rows(out_ref, out)
            put_rows(gs_ref, g * a1)
            delta = jnp.sum(gs.astype(F32) * out.astype(F32), axis=1, keepdims=True)
            ds = (p * (dot_nt(gs, kv_ref[keys, HD:]) - delta)).astype(BF16)
            put_rows(dq_ref, dot_nn(ds, k) * SCALE)
            add_grads(dk_s, dv_s, first, w, dot_nn(jnp.transpose(q), ds), dot_nn(jnp.transpose(gs), pb))

    @pl.when(i == tiles - 1)
    def _():
        write_grads(dkv_ref, dk_s, dv_s)


def add_grads(dk_s, dv_s, first, count, dk, dv):
    for j in range(count):
        dk_s[first + j] += dk[:, j * TILE:(j + 1) * TILE]
        dv_s[first + j] += dv[:, j * TILE:(j + 1) * TILE]


def write_grads(ref, dk_s, dv_s):
    for j in range(dk_s.shape[0]):
        at = slice(j * TILE, (j + 1) * TILE)
        ref[at, :HD] = (jnp.transpose(dk_s[j]) * SCALE).astype(ref.dtype)
        ref[at, HD:] = jnp.transpose(dv_s[j]).astype(ref.dtype)


def local_backward(n_ref, q_ref, gs_ref, out_ref, p_ref, dqp_ref, kv_ref, dq_ref, dkv_ref, dk_s, dv_s):
    i = pl.program_id(0)
    tiles = pl.num_programs(0)
    rows = kv_ref.shape[0]

    @pl.when(i == 0)
    def _():
        dk_s[...] = jnp.zeros_like(dk_s)
        dv_s[...] = jnp.zeros_like(dv_s)

    for w in range(1, rows // TILE + 1):
        @pl.when(n_ref[i] == w)
        def _(w=w):
            first = i - (w - 1)
            keys = pl.ds(pl.multiple_of(first * TILE, TILE), w * TILE)
            q = by_rows(q_ref)
            gs = by_rows(gs_ref)
            pb = p_ref[0, :, :w * TILE]
            delta = jnp.sum(gs.astype(F32) * by_rows(out_ref).astype(F32), axis=1, keepdims=True)
            ds = (pb.astype(F32) * (dot_nt(gs, kv_ref[keys, HD:]) - delta)).astype(BF16)
            put_rows(dq_ref, dot_nn(ds, kv_ref[keys, :HD]) * SCALE)
            add_grads(dk_s, dv_s, first, w, dot_nn(jnp.transpose(q), ds), dot_nn(jnp.transpose(gs), pb))

    @pl.when(n_ref[tiles + i] > 0)
    def _():
        dq_ref[...] = (dq_ref[...].astype(F32) + dqp_ref[...].astype(F32)).astype(BF16)

    @pl.when(i == tiles - 1)
    def _():
        write_grads(dkv_ref, dk_s, dv_s)


def call(body, name, rows, ins, outs, scratch, flops, aliases={}):
    tiles = rows // TILE
    big = rows * 4 * HD
    run = pl.pallas_call(
        body,
        grid_spec=pltpu.PrefetchScalarGridSpec(
            num_scalar_prefetch=1, grid=(tiles,), in_specs=ins, out_specs=[s for s, _ in outs], scratch_shapes=scratch
        ),
        out_shape=[s if math.prod(s.shape) < big else pltpu.HBM(s.shape, s.dtype) for _, s in outs],
        input_output_aliases=aliases,
        compiler_params=pltpu.CompilerParams(dimension_semantics=("arbitrary",), vmem_limit_bytes=40 << 20),
        cost_estimate=pl.CostEstimate(flops=flops, transcendentals=0, bytes_accessed=8 << 20),
        name=name,
    )
    return lambda n, *args: run(n, *[x if x.size < big else pltpu.with_memory_space_constraint(x, pltpu.HBM) for x in args])


def attention_calls(counts, starts, q, g, rows, width):
    tiles = rows // TILE
    sds = jax.ShapeDtypeStruct
    own_tile = lambda i, n: i
    met_tile = lambda i, n: jnp.minimum(i, jnp.maximum(n[2 * tiles] - 1, 0))
    whole = pl.BlockSpec((rows, 2 * HD), lambda i, n: (0, 0))

    def flat(at, w=width):
        return pl.BlockSpec((TILE, w), lambda i, n: (at(i, n), 0))

    def slab(at, *dims):
        return pl.BlockSpec((1,) + dims, lambda i, n: (at(i, n), 0, 0))

    grads = [pltpu.VMEM((tiles, HD, TILE), F32)] * 2
    shared = [pltpu.VMEM((rows, 2 * HD), BF16), pltpu.VMEM((TILE, rows), F32)]
    rows_bf16 = sds((rows, width), BF16)

    def forward_local(own):
        return call(
            local_forward, "local_forward", rows,
            [slab(own_tile, 1, TILE), flat(own_tile), flat(own_tile), whole],
            [
                (slab(own_tile, width, rows), sds((tiles, width, rows), BF16)),
                (slab(own_tile, width, 2 * HD), sds((tiles, width, 2 * HD), F32)),
                (slab(own_tile, width, HD), sds((tiles, width, HD), F32)),
                (flat(own_tile), rows_bf16),
                (flat(own_tile), rows_bf16),
            ],
            shared, 3 << 30,
        )(counts, starts, q, g, own)

    def finish_prev(prev, o, maxes, out, gs):
        return call(
            prev_step, "previous_block", rows,
            [
                slab(met_tile, 1, TILE), flat(met_tile), flat(met_tile), whole,
                slab(met_tile, width, 2 * HD), slab(met_tile, width, HD), flat(met_tile), flat(met_tile),
            ],
            [
                (flat(met_tile), rows_bf16), (flat(met_tile), rows_bf16), (flat(met_tile), rows_bf16),
                (whole, sds((rows, 2 * HD), BF16)),
            ],
            shared + grads, 4 << 30, {7: 0, 8: 1},
        )(counts, starts, q, g, prev, o, maxes, out, gs)

    def backward_local(gs, out, p, dqp, own):
        return call(
            local_backward, "local_backward", rows,
            [flat(own_tile), flat(own_tile), flat(own_tile), slab(own_tile, width, rows), flat(met_tile), whole],
            [(flat(own_tile), rows_bf16), (whole, sds((rows, 2 * HD), F32))],
            grads, 5 << 30,
        )(counts, q, gs, out, p, dqp, own)

    return forward_local, finish_prev, backward_local


def passed_along(x, axis, by):
    count = lax.axis_size(axis)
    pairs = [(i, i + by) for i in range(count) if 0 <= i + by < count]
    return lax.ppermute(x, axis, pairs)


def by_head(x):
    return jnp.transpose(x.reshape(x.shape[0], -1, HD), (1, 0, 2))


def by_token(x):
    return jnp.transpose(x, (1, 0, 2)).reshape(x.shape[1], -1)


def per_device(queries, keys, values, grad_out, doc_lengths):
    rows = queries.shape[0]
    shared = jnp.concatenate([by_head(keys), by_head(values)], axis=2)
    own = lax.all_to_all(shared, "dp", split_axis=0, concat_axis=0, tiled=True).reshape(rows, 2 * HD)
    prev = passed_along(own, "ctx", 1)
    first_pos = lax.axis_index("ctx") * rows
    ends = jnp.cumsum(doc_lengths)
    positions = first_pos + jnp.arange(rows, dtype=jnp.int32)
    starts = jnp.max(jnp.where(ends[None, :] <= positions[:, None], ends[None, :], 0), axis=1)
    starts = (starts - first_pos + rows).astype(jnp.int32)
    tiles = rows // TILE
    index = jnp.arange(tiles, dtype=jnp.int32)
    all_tiles = index + tiles - starts[::TILE] // TILE + 1
    here = jnp.minimum(all_tiles, index + 1)
    before = all_tiles - here
    counts = jnp.concatenate([here, before, jnp.sum(before > 0, dtype=jnp.int32)[None]])
    forward_local, finish_prev, backward_local = attention_calls(
        counts, starts.reshape(tiles, 1, TILE), queries, grad_out, rows, queries.shape[1]
    )
    probs, sums, maxes, out, scaled = forward_local(own)
    attn_out, scaled, grad_q_prev, back = finish_prev(prev, sums, maxes, out, scaled)
    grad_q, mine = backward_local(scaled, attn_out, probs, grad_q_prev, own)
    total = (mine + passed_along(back, "ctx", -1).astype(F32)).astype(BF16)
    total = total.reshape(shared.shape)
    grads = lax.all_to_all(total, "dp", split_axis=0, concat_axis=0, tiled=True)
    return attn_out, grad_q, by_token(grads[:, :, :HD]), by_token(grads[:, :, HD:])


def solution(mesh):
    placed = (P("ctx", "dp"), P(("ctx", "dp"), None), P(("ctx", "dp"), None), P("ctx", "dp"), P())
    return jax.shard_map(
        per_device,
        mesh=mesh,
        in_specs=placed,
        out_specs=(P("ctx", "dp"), P("ctx", "dp"), P(("ctx", "dp"), None), P(("ctx", "dp"), None)),
        check_vma=False,
    )
```

```python
import functools
import math

import jax
import jax.numpy as jnp
from jax import lax
from jax.experimental import pallas as pl
from jax.experimental.pallas import tpu as pltpu
from jax.sharding import PartitionSpec as P

HD = 128
TILE = 128
NEG = -1e30
F32 = jnp.float32
BF16 = jnp.bfloat16
SCALE = 1.0 / math.sqrt(HD)
LOG2_SCALE = SCALE * math.log2(math.e)


def dot_nt(a, b):
    return lax.dot_general(a, b, (((1,), (1,)), ((), ())), preferred_element_type=F32)


def dot_nn(a, b):
    return lax.dot_general(a, b, (((1,), (0,)), ((), ())), preferred_element_type=F32)


def by_rows(ref):
    return jnp.concatenate([ref[:, h * HD:(h + 1) * HD] for h in range(ref.shape[1] // HD)], axis=0)


def put_rows(ref, x):
    for h in range(ref.shape[1] // HD):
        ref[:, h * HD:(h + 1) * HD] = x[h * TILE:(h + 1) * TILE].astype(ref.dtype)


def write_bias(bias_ref, start_ref, first, count, offset, causal):
    startc = jnp.transpose(jnp.broadcast_to(start_ref[0], (TILE, TILE)))
    lane = lax.broadcasted_iota(jnp.int32, (TILE, TILE), 1)
    row = lax.broadcasted_iota(jnp.int32, (TILE, TILE), 0)
    for j in range(count):
        keep = lane >= startc - ((first + j) * TILE + offset)
        if causal and j == count - 1:
            keep = keep & (lane <= row)
        bias_ref[:, j * TILE:(j + 1) * TILE] = jnp.where(keep, 0.0, NEG)


def biased_scores(q, k, bias, heads):
    t = dot_nt(q, k) * LOG2_SCALE
    rows, width = t.shape
    return (t.reshape(heads, TILE, width) + bias[None]).reshape(rows, width)


def key_tiles(first_ref, i, tiles):
    first = lax.div(first_ref[i], TILE)
    return jnp.minimum(tiles + i - first, i) + 1, jnp.maximum(tiles - first, 0)


def crossing_tiles(first_ref, tiles):
    total = jnp.int32(0)
    for i in range(tiles):
        total = total + (first_ref[i] < tiles * TILE).astype(jnp.int32)
    return total


def local_forward(first_ref, start_ref, q_ref, g_ref, kv_ref, p_ref, o_ref, max_ref, out_ref, gs_ref, v_s, bias_s):
    i = pl.program_id(0)
    tiles = pl.num_programs(0)
    rows = kv_ref.shape[0]
    heads = q_ref.shape[1] // HD
    here, before = key_tiles(first_ref, i, tiles)

    @pl.when(i == 0)
    def _():
        v_s[:, :HD] = kv_ref[:, HD:]
        v_s[:, HD:] = jnp.ones((rows, HD), BF16)

    for w in range(1, rows // TILE + 1):
        @pl.when(here == w)
        def _(w=w):
            first = i - (w - 1)
            write_bias(bias_s, start_ref, first, w, rows, True)
            keys = pl.ds(pl.multiple_of(first * TILE, TILE), w * TILE)
            t = biased_scores(by_rows(q_ref), kv_ref[keys, :HD], bias_s[:, :w * TILE], heads)
            m = jnp.max(t, axis=1, keepdims=True)
            p = jnp.exp2(t - m).astype(BF16)
            p_ref[i, :, :w * TILE] = p
            o_ref[i] = dot_nn(p, v_s[keys, :])
            max_ref[i] = jnp.broadcast_to(m, max_ref.shape[1:])

    @pl.when(before == 0)
    def _():
        inv = 1.0 / o_ref[i, :, HD:]
        put_rows(out_ref, o_ref[i, :, :HD] * inv)
        put_rows(gs_ref, by_rows(g_ref).astype(F32) * inv)


def prev_step(first_ref, start_ref, q_ref, g_ref, kv_ref, o_ref, max_ref, out_in_ref, gs_in_ref,
              out_ref, gs_ref, dq_ref, dkv_ref, v_s, bias_s, dk_s, dv_s):
    i = pl.program_id(0)
    rows = kv_ref.shape[0]
    tiles = rows // TILE
    heads = q_ref.shape[1] // HD
    before = key_tiles(first_ref, i, tiles)[1]

    @pl.when(i == 0)
    def _():
        v_s[:, :HD] = kv_ref[:, HD:]
        v_s[:, HD:] = jnp.ones((rows, HD), BF16)
        dk_s[...] = jnp.zeros_like(dk_s)
        dv_s[...] = jnp.zeros_like(dv_s)

    @pl.when((i == 0) & (before == 0))
    def _():
        out_ref[...] = out_in_ref[...]
        gs_ref[...] = gs_in_ref[...]
        dq_ref[...] = jnp.zeros_like(dq_ref)

    for w in range(1, rows // TILE + 1):
        @pl.when(before == w)
        def _(w=w):
            first = rows // TILE - w
            write_bias(bias_s, start_ref, first, w, 0, False)
            keys = slice(first * TILE, rows)
            q = by_rows(q_ref)
            g = by_rows(g_ref).astype(F32)
            k = kv_ref[keys, :HD]
            t = biased_scores(q, k, bias_s[:, :w * TILE], heads)
            m1 = max_ref[i]
            m = jnp.maximum(m1, jnp.max(t, axis=1, keepdims=True))
            a1 = jnp.exp2(m1 - m)
            p = jnp.exp2(t - jnp.concatenate([m] * w, axis=1))
            pb = p.astype(BF16)
            o2 = dot_nn(pb, v_s[keys, :])
            inv = 1.0 / (a1 * o_ref[i, :, HD:] + o2[:, HD:])
            out = ((a1 * o_ref[i, :, :HD] + o2[:, :HD]) * inv).astype(BF16)
            g = g * inv
            gs = g.astype(BF16)
            put_rows(out_ref, out)
            put_rows(gs_ref, g * a1)
            delta = jnp.sum(gs.astype(F32) * out.astype(F32), axis=1, keepdims=True)
            ds = (p * (dot_nt(gs, kv_ref[keys, HD:]) - delta)).astype(BF16)
            put_rows(dq_ref, dot_nn(ds, k) * SCALE)
            add_grads(dk_s, dv_s, first, w, dot_nn(jnp.transpose(q), ds), dot_nn(jnp.transpose(gs), pb))

    @pl.when(i == pl.num_programs(0) - 1)
    def _():
        write_grads(dkv_ref, dk_s, dv_s)


def add_grads(dk_s, dv_s, first, count, dk, dv):
    for j in range(count):
        dk_s[first + j] += dk[:, j * TILE:(j + 1) * TILE]
        dv_s[first + j] += dv[:, j * TILE:(j + 1) * TILE]


def write_grads(ref, dk_s, dv_s):
    for j in range(dk_s.shape[0]):
        at = slice(j * TILE, (j + 1) * TILE)
        ref[at, :HD] = (jnp.transpose(dk_s[j]) * SCALE).astype(ref.dtype)
        ref[at, HD:] = jnp.transpose(dv_s[j]).astype(ref.dtype)


def local_backward(first_ref, q_ref, gs_ref, out_ref, p_ref, dqp_ref, kv_ref, dq_ref, dkv_ref, dk_s, dv_s):
    i = pl.program_id(0)
    tiles = pl.num_programs(0)
    rows = kv_ref.shape[0]
    here, before = key_tiles(first_ref, i, tiles)

    @pl.when(i == 0)
    def _():
        dk_s[...] = jnp.zeros_like(dk_s)
        dv_s[...] = jnp.zeros_like(dv_s)

    for w in range(1, rows // TILE + 1):
        @pl.when(here == w)
        def _(w=w):
            first = i - (w - 1)
            keys = pl.ds(pl.multiple_of(first * TILE, TILE), w * TILE)
            q = by_rows(q_ref)
            gs = by_rows(gs_ref)
            pb = p_ref[i, :, :w * TILE]
            delta = jnp.sum(gs.astype(F32) * by_rows(out_ref).astype(F32), axis=1, keepdims=True)
            ds = (pb.astype(F32) * (dot_nt(gs, kv_ref[keys, HD:]) - delta)).astype(BF16)
            put_rows(dq_ref, dot_nn(ds, kv_ref[keys, :HD]) * SCALE)
            add_grads(dk_s, dv_s, first, w, dot_nn(jnp.transpose(q), ds), dot_nn(jnp.transpose(gs), pb))

    @pl.when(before > 0)
    def _():
        dq_ref[...] = (dq_ref[...].astype(F32) + dqp_ref[...].astype(F32)).astype(BF16)

    @pl.when(i == tiles - 1)
    def _():
        write_grads(dkv_ref, dk_s, dv_s)


def call(body, name, rows, steps, ins, outs, scratch, flops, limit, aliases={}):
    big = rows * 4 * HD

    def in_hbm(x):
        if isinstance(x, jax.ShapeDtypeStruct) and math.prod(x.shape) >= big:
            return pltpu.HBM(x.shape, x.dtype)
        return x

    run = pl.pallas_call(
        body,
        grid_spec=pltpu.PrefetchScalarGridSpec(
            num_scalar_prefetch=1, grid=(steps,), in_specs=ins, out_specs=[s for s, _ in outs], scratch_shapes=scratch
        ),
        out_shape=[in_hbm(s) for _, s in outs],
        input_output_aliases=aliases,
        compiler_params=pltpu.CompilerParams(dimension_semantics=("arbitrary",), vmem_limit_bytes=limit << 20),
        cost_estimate=pl.CostEstimate(flops=flops, transcendentals=0, bytes_accessed=8 << 20),
        name=name,
    )
    return lambda n, *args: run(n, *[pltpu.with_memory_space_constraint(x, pltpu.HBM) if x.ndim == 2 and x.size >= big else x for x in args])


def attention_calls(first, starts, q, g):
    rows, width = q.shape
    tiles = rows // TILE
    sds = jax.ShapeDtypeStruct
    own_tile = lambda i, n: i
    met_tile = lambda i, n: jnp.minimum(i, jnp.maximum(crossing_tiles(n, tiles) - 1, 0))
    whole = pl.BlockSpec((rows, 2 * HD), lambda i, n: (0, 0))

    def flat(at, w=width):
        return pl.BlockSpec((TILE, w), lambda i, n: (at(i, n), 0))

    def slab(at, *dims):
        return pl.BlockSpec((1,) + dims, lambda i, n: (at(i, n), 0, 0))

    held = pl.BlockSpec(memory_space=pltpu.VMEM)
    grads = [pltpu.VMEM((tiles, HD, TILE), F32)] * 2
    shared = [pltpu.VMEM((rows, 2 * HD), BF16), pltpu.VMEM((TILE, rows), F32)]
    rows_bf16 = sds((rows, width), BF16)

    def forward_local(own):
        return call(
            local_forward, "local_forward", rows, tiles,
            [slab(own_tile, 1, TILE), flat(own_tile), flat(own_tile), whole],
            [
                (held, pltpu.VMEM((tiles, width, rows), BF16)),
                (held, pltpu.VMEM((tiles, width, 2 * HD), F32)),
                (held, pltpu.VMEM((tiles, width, HD), F32)),
                (flat(own_tile), rows_bf16),
                (flat(own_tile), rows_bf16),
            ],
            shared, 3 << 30, 28,
        )(first, starts, q, g, own)

    def finish_prev(prev, o, maxes, out, gs):
        return call(
            prev_step, "previous_block", rows, tiles,
            [
                slab(met_tile, 1, TILE), flat(met_tile), flat(met_tile), whole,
                held, held, flat(met_tile), flat(met_tile),
            ],
            [
                (flat(met_tile), rows_bf16), (flat(met_tile), rows_bf16), (flat(met_tile), rows_bf16),
                (whole, sds((rows, 2 * HD), BF16)),
            ],
            shared + grads, 4 << 30, 28, {7: 0, 8: 1},
        )(first, starts, q, g, prev, o, maxes, out, gs)

    def backward_local(gs, out, p, dqp, own):
        return call(
            local_backward, "local_backward", rows, tiles,
            [flat(own_tile), flat(own_tile), flat(own_tile), held, flat(met_tile), whole],
            [(flat(own_tile), rows_bf16), (whole, sds((rows, 2 * HD), F32))],
            grads, 5 << 30, 28,
        )(first, q, gs, out, p, dqp, own)

    return forward_local, finish_prev, backward_local


def pack_kernel(k_ref, v_ref, out_ref):
    for h in range(out_ref.shape[0]):
        out_ref[h, :, :HD] = k_ref[:, h * HD:(h + 1) * HD]
        out_ref[h, :, HD:] = v_ref[:, h * HD:(h + 1) * HD]


def unpack_kernel(x_ref, k_ref, v_ref):
    for h in range(x_ref.shape[0]):
        k_ref[:, h * HD:(h + 1) * HD] = x_ref[h, :, :HD]
        v_ref[:, h * HD:(h + 1) * HD] = x_ref[h, :, HD:]


def pack(keys, values):
    tokens, width = keys.shape
    return pl.pallas_call(
        pack_kernel, out_shape=jax.ShapeDtypeStruct((width // HD, tokens, 2 * HD), BF16), name="pack_heads"
    )(keys, values)


def unpack(x):
    heads, tokens, _ = x.shape
    return pl.pallas_call(
        unpack_kernel, out_shape=[jax.ShapeDtypeStruct((tokens, heads * HD), BF16)] * 2, name="unpack_heads"
    )(x)


def passed_along(x, axis, by):
    count = lax.axis_size(axis)
    pairs = [(i, (i + by) % count) for i in range(count)]
    return lax.ppermute(x, axis, pairs)


def per_device(queries, keys, values, grad_out, doc_lengths):
    rows = queries.shape[0]
    shared = pack(keys, values)
    own = lax.all_to_all(shared, "dp", split_axis=0, concat_axis=0, tiled=True).reshape(rows, 2 * HD)
    first_pos = lax.axis_index("ctx") * rows
    ends = jnp.cumsum(doc_lengths)
    positions = first_pos + jnp.arange(rows, dtype=jnp.int32)
    starts = jnp.max(jnp.where(ends[None, :] <= positions[:, None], ends[None, :], 0), axis=1)
    starts = (starts - first_pos + rows).astype(jnp.int32)
    tiles = rows // TILE
    first = starts[::TILE]
    own, first = lax.optimization_barrier((own, first))
    prev = passed_along(own, "ctx", 1)
    forward_local, finish_prev, backward_local = attention_calls(
        first, starts.reshape(tiles, 1, TILE), queries, grad_out
    )
    probs, sums, maxes, out, scaled = forward_local(own)
    attn_out, scaled, grad_q_prev, back = finish_prev(prev, sums, maxes, out, scaled)
    grad_q, mine = backward_local(scaled, attn_out, probs, grad_q_prev, own)
    total = (mine + passed_along(back, "ctx", -1).astype(F32)).astype(BF16)
    total = total.reshape(shared.shape)
    grads = lax.all_to_all(total, "dp", split_axis=0, concat_axis=0, tiled=True)
    grad_k, grad_v = unpack(grads)
    return attn_out, grad_q, grad_k, grad_v


def solution(mesh):
    placed = (P("ctx", "dp"), P(("ctx", "dp"), None), P(("ctx", "dp"), None), P("ctx", "dp"), P())
    return jax.shard_map(
        per_device,
        mesh=mesh,
        in_specs=placed,
        out_specs=(P("ctx", "dp"), P("ctx", "dp"), P(("ctx", "dp"), None), P(("ctx", "dp"), None)),
        check_vma=False,
    )
```

```python
import functools
import math

import jax
import jax.numpy as jnp
from jax import lax
from jax.experimental import pallas as pl
from jax.experimental.pallas import tpu as pltpu
from jax.sharding import PartitionSpec as P

HD = 128
TILE = 128
NEG = -1e30
F32 = jnp.float32
BF16 = jnp.bfloat16
SCALE = 1.0 / math.sqrt(HD)
LOG2_SCALE = SCALE * math.log2(math.e)


def dot_nt(a, b):
    return lax.dot_general(a, b, (((1,), (1,)), ((), ())), preferred_element_type=F32)


def dot_nn(a, b):
    return lax.dot_general(a, b, (((1,), (0,)), ((), ())), preferred_element_type=F32)


def by_rows(ref):
    return jnp.concatenate([ref[:, h * HD:(h + 1) * HD] for h in range(ref.shape[1] // HD)], axis=0)


def put_rows(ref, x):
    for h in range(ref.shape[1] // HD):
        ref[:, h * HD:(h + 1) * HD] = x[h * TILE:(h + 1) * TILE].astype(ref.dtype)


def write_bias(bias_ref, start_ref, first, count, offset, causal):
    startc = jnp.transpose(jnp.broadcast_to(start_ref[0], (TILE, TILE)))
    lane = lax.broadcasted_iota(jnp.int32, (TILE, TILE), 1)
    row = lax.broadcasted_iota(jnp.int32, (TILE, TILE), 0)
    for j in range(count):
        keep = lane >= startc - ((first + j) * TILE + offset)
        if causal and j == count - 1:
            keep = keep & (lane <= row)
        bias_ref[:, j * TILE:(j + 1) * TILE] = jnp.where(keep, 0.0, NEG)


def biased_scores(q, k, bias, heads):
    t = dot_nt(q, k) * LOG2_SCALE
    rows, width = t.shape
    return (t.reshape(heads, TILE, width) + bias[None]).reshape(rows, width)


def key_tiles(first_ref, i, tiles):
    first = lax.div(first_ref[i], TILE)
    return jnp.minimum(tiles + i - first, i) + 1, jnp.maximum(tiles - first, 0)


def local_forward(first_ref, start_ref, q_ref, g_ref, kv_ref, p_ref, o_ref, max_ref, out_ref, gs_ref, v_s, bias_s):
    i = pl.program_id(0)
    tiles = pl.num_programs(0)
    rows = kv_ref.shape[0]
    heads = q_ref.shape[1] // HD
    here, before = key_tiles(first_ref, i, tiles)

    @pl.when(i == 0)
    def _():
        v_s[:, :HD] = kv_ref[:, HD:]
        v_s[:, HD:] = jnp.ones((rows, HD), BF16)

    for w in range(1, rows // TILE + 1):
        @pl.when(here == w)
        def _(w=w):
            first = i - (w - 1)
            write_bias(bias_s, start_ref, first, w, rows, True)
            keys = pl.ds(pl.multiple_of(first * TILE, TILE), w * TILE)
            t = biased_scores(by_rows(q_ref), kv_ref[keys, :HD], bias_s[:, :w * TILE], heads)
            m = jnp.max(t, axis=1, keepdims=True)
            p = jnp.exp2(t - m).astype(BF16)
            p_ref[i, :, :w * TILE] = p
            o_ref[i] = dot_nn(p, v_s[keys, :])
            max_ref[i] = jnp.broadcast_to(m, max_ref.shape[1:])

    @pl.when(before == 0)
    def _():
        finish_rows(o_ref, g_ref, out_ref, gs_ref, i)


def finish_rows(o_ref, g_ref, out_ref, gs_ref, i):
    inv = 1.0 / o_ref[i, :, HD:]
    put_rows(out_ref, o_ref[i, :, :HD] * inv)
    put_rows(gs_ref, by_rows(g_ref).astype(F32) * inv)


def prev_step(first_ref, start_ref, q_ref, g_ref, kv_ref, o_ref, max_ref, out_any, gs_any,
              out_ref, gs_ref, dq_ref, dkv_ref, v_s, bias_s, dk_s, dv_s):
    i = pl.program_id(0)
    rows = kv_ref.shape[0]
    tiles = rows // TILE
    heads = q_ref.shape[1] // HD
    before = key_tiles(first_ref, i, tiles)[1]

    @pl.when(i == 0)
    def _():
        v_s[:, :HD] = kv_ref[:, HD:]
        v_s[:, HD:] = jnp.ones((rows, HD), BF16)
        dk_s[...] = jnp.zeros_like(dk_s)
        dv_s[...] = jnp.zeros_like(dv_s)

    @pl.when((i == 0) & (before == 0))
    def _():
        finish_rows(o_ref, g_ref, out_ref, gs_ref, 0)
        dq_ref[...] = jnp.zeros_like(dq_ref)

    for w in range(1, rows // TILE + 1):
        @pl.when(before == w)
        def _(w=w):
            first = rows // TILE - w
            write_bias(bias_s, start_ref, first, w, 0, False)
            keys = slice(first * TILE, rows)
            q = by_rows(q_ref)
            g = by_rows(g_ref).astype(F32)
            k = kv_ref[keys, :HD]
            t = biased_scores(q, k, bias_s[:, :w * TILE], heads)
            m1 = max_ref[i]
            m = jnp.maximum(m1, jnp.max(t, axis=1, keepdims=True))
            a1 = jnp.exp2(m1 - m)
            p = jnp.exp2(t - jnp.concatenate([m] * w, axis=1))
            pb = p.astype(BF16)
            o2 = dot_nn(pb, v_s[keys, :])
            inv = 1.0 / (a1 * o_ref[i, :, HD:] + o2[:, HD:])
            out = ((a1 * o_ref[i, :, :HD] + o2[:, :HD]) * inv).astype(BF16)
            g = g * inv
            gs = g.astype(BF16)
            put_rows(out_ref, out)
            put_rows(gs_ref, g * a1)
            delta = jnp.sum(gs.astype(F32) * out.astype(F32), axis=1, keepdims=True)
            ds = (p * (dot_nt(gs, kv_ref[keys, HD:]) - delta)).astype(BF16)
            put_rows(dq_ref, dot_nn(ds, k) * SCALE)
            add_grads(dk_s, dv_s, first, w, dot_nn(jnp.transpose(q), ds), dot_nn(jnp.transpose(gs), pb))

    @pl.when(i == pl.num_programs(0) - 1)
    def _():
        write_grads(dkv_ref, dk_s, dv_s)


def add_grads(dk_s, dv_s, first, count, dk, dv):
    for j in range(count):
        dk_s[first + j] += dk[:, j * TILE:(j + 1) * TILE]
        dv_s[first + j] += dv[:, j * TILE:(j + 1) * TILE]


def write_grads(ref, dk_s, dv_s):
    for j in range(dk_s.shape[0]):
        at = slice(j * TILE, (j + 1) * TILE)
        ref[at, :HD] = (jnp.transpose(dk_s[j]) * SCALE).astype(ref.dtype)
        ref[at, HD:] = jnp.transpose(dv_s[j]).astype(ref.dtype)


def local_backward(first_ref, q_ref, gs_ref, out_ref, p_ref, dqp_ref, kv_ref, dq_ref, dkv_ref, dk_s, dv_s):
    i = pl.program_id(0)
    tiles = pl.num_programs(0)
    rows = kv_ref.shape[0]
    here, before = key_tiles(first_ref, i, tiles)

    @pl.when(i == 0)
    def _():
        dk_s[...] = jnp.zeros_like(dk_s)
        dv_s[...] = jnp.zeros_like(dv_s)

    for w in range(1, rows // TILE + 1):
        @pl.when(here == w)
        def _(w=w):
            first = i - (w - 1)
            keys = pl.ds(pl.multiple_of(first * TILE, TILE), w * TILE)
            q = by_rows(q_ref)
            gs = by_rows(gs_ref)
            pb = p_ref[i, :, :w * TILE]
            delta = jnp.sum(gs.astype(F32) * by_rows(out_ref).astype(F32), axis=1, keepdims=True)
            ds = (pb.astype(F32) * (dot_nt(gs, kv_ref[keys, HD:]) - delta)).astype(BF16)
            put_rows(dq_ref, dot_nn(ds, kv_ref[keys, :HD]) * SCALE)
            add_grads(dk_s, dv_s, first, w, dot_nn(jnp.transpose(q), ds), dot_nn(jnp.transpose(gs), pb))

    @pl.when(before > 0)
    def _():
        dq_ref[...] = (dq_ref[...].astype(F32) + dqp_ref[...].astype(F32)).astype(BF16)

    @pl.when(i == tiles - 1)
    def _():
        write_grads(dkv_ref, dk_s, dv_s)


def call(body, name, rows, steps, ins, outs, scratch, flops, limit, aliases={}):
    big = rows * 4 * HD

    def in_hbm(x):
        if isinstance(x, jax.ShapeDtypeStruct) and math.prod(x.shape) >= big:
            return pltpu.HBM(x.shape, x.dtype)
        return x

    run = pl.pallas_call(
        body,
        grid_spec=pltpu.PrefetchScalarGridSpec(
            num_scalar_prefetch=1, grid=(steps,), in_specs=ins, out_specs=[s for s, _ in outs], scratch_shapes=scratch
        ),
        out_shape=[in_hbm(s) for _, s in outs],
        input_output_aliases=aliases,
        compiler_params=pltpu.CompilerParams(dimension_semantics=("arbitrary",), vmem_limit_bytes=limit << 20),
        cost_estimate=pl.CostEstimate(flops=flops, transcendentals=0, bytes_accessed=8 << 20),
        name=name,
    )
    return lambda n, *args: run(n, *[pltpu.with_memory_space_constraint(x, pltpu.HBM) if x.ndim == 2 and x.size >= big else x for x in args])


def attention_calls(first, starts, q, g):
    rows, width = q.shape
    tiles = rows // TILE
    sds = jax.ShapeDtypeStruct
    own_tile = lambda i, n: i
    met_tile = lambda i, n: n[tiles + i]
    whole = pl.BlockSpec((rows, 2 * HD), lambda i, n: (0, 0))

    def flat(at, w=width):
        return pl.BlockSpec((TILE, w), lambda i, n: (at(i, n), 0))

    def slab(at, *dims):
        return pl.BlockSpec((1,) + dims, lambda i, n: (at(i, n), 0, 0))

    held = pl.BlockSpec(memory_space=pltpu.VMEM)
    there = pl.BlockSpec(memory_space=pl.ANY)
    grads = [pltpu.VMEM((tiles, HD, TILE), F32)] * 2
    shared = [pltpu.VMEM((rows, 2 * HD), BF16), pltpu.VMEM((TILE, rows), F32)]
    rows_bf16 = sds((rows, width), BF16)

    def forward_local(own):
        return call(
            local_forward, "local_forward", rows, tiles,
            [slab(own_tile, 1, TILE), flat(own_tile), flat(own_tile), whole],
            [
                (held, pltpu.VMEM((tiles, width, rows), BF16)),
                (held, pltpu.VMEM((tiles, width, 2 * HD), F32)),
                (held, pltpu.VMEM((tiles, width, HD), F32)),
                (flat(own_tile), rows_bf16),
                (flat(own_tile), rows_bf16),
            ],
            shared, 3 << 30, 28,
        )(first, starts, q, g, own)

    def finish_prev(prev, o, maxes, out, gs):
        return call(
            prev_step, "previous_block", rows, tiles,
            [
                slab(met_tile, 1, TILE), flat(met_tile), flat(met_tile), whole,
                held, held, there, there,
            ],
            [
                (flat(met_tile), rows_bf16), (flat(met_tile), rows_bf16), (flat(met_tile), rows_bf16),
                (whole, sds((rows, 2 * HD), BF16)),
            ],
            shared + grads, 4 << 30, 28, {7: 0, 8: 1},
        )(first, starts, q, g, prev, o, maxes, out, gs)

    def backward_local(gs, out, p, dqp, own):
        return call(
            local_backward, "local_backward", rows, tiles,
            [flat(own_tile), flat(own_tile), flat(own_tile), held, flat(met_tile), whole],
            [(flat(own_tile), rows_bf16), (whole, sds((rows, 2 * HD), F32))],
            grads, 5 << 30, 28,
        )(first, q, gs, out, p, dqp, own)

    return forward_local, finish_prev, backward_local


def pack_kernel(k_ref, v_ref, out_ref):
    for h in range(out_ref.shape[0]):
        out_ref[h, :, :HD] = k_ref[:, h * HD:(h + 1) * HD]
        out_ref[h, :, HD:] = v_ref[:, h * HD:(h + 1) * HD]


def unpack_kernel(x_ref, k_ref, v_ref):
    for h in range(x_ref.shape[0]):
        k_ref[:, h * HD:(h + 1) * HD] = x_ref[h, :, :HD]
        v_ref[:, h * HD:(h + 1) * HD] = x_ref[h, :, HD:]


def pack(keys, values):
    tokens, width = keys.shape
    return pl.pallas_call(
        pack_kernel, out_shape=jax.ShapeDtypeStruct((width // HD, tokens, 2 * HD), BF16), name="pack_heads"
    )(keys, values)


def unpack(x):
    heads, tokens, _ = x.shape
    return pl.pallas_call(
        unpack_kernel,
        in_specs=[pl.BlockSpec(memory_space=pltpu.VMEM)],
        out_shape=[jax.ShapeDtypeStruct((tokens, heads * HD), BF16)] * 2,
        name="unpack_heads",
    )(pltpu.with_memory_space_constraint(x, pltpu.VMEM))


def passed_along(x, axis, by, ring):
    count = lax.axis_size(axis)
    pairs = [(i, (i + by) % count) for i in range(count) if ring or 0 <= i + by < count]
    return lax.ppermute(x, axis, pairs)


def per_device(queries, keys, values, grad_out, doc_lengths):
    rows = queries.shape[0]
    shared = pack(keys, values)
    own = lax.all_to_all(shared, "dp", split_axis=0, concat_axis=0, tiled=True).reshape(rows, 2 * HD)
    first_pos = lax.axis_index("ctx") * rows
    ends = jnp.cumsum(doc_lengths)
    positions = first_pos + jnp.arange(rows, dtype=jnp.int32)
    starts = jnp.max(jnp.where(ends[None, :] <= positions[:, None], ends[None, :], 0), axis=1)
    starts = (starts - first_pos + rows).astype(jnp.int32)
    tiles = rows // TILE
    first = starts[::TILE]
    crossing = jnp.sum(first < rows, dtype=jnp.int32)
    met = jnp.minimum(jnp.arange(tiles, dtype=jnp.int32), jnp.maximum(crossing - 1, 0))
    first = jnp.concatenate([first, met])
    own, first = lax.optimization_barrier((own, first))
    prev = passed_along(own, "ctx", 1, True)
    forward_local, finish_prev, backward_local = attention_calls(
        first, starts.reshape(tiles, 1, TILE), queries, grad_out
    )
    probs, sums, maxes, out, scaled = forward_local(own)
    attn_out, scaled, grad_q_prev, back = finish_prev(prev, sums, maxes, out, scaled)
    grad_q, mine = backward_local(scaled, attn_out, probs, grad_q_prev, own)
    total = (mine + passed_along(back, "ctx", -1, False).astype(F32)).astype(BF16)
    total = total.reshape(shared.shape)
    grads = lax.all_to_all(total, "dp", split_axis=0, concat_axis=0, tiled=True)
    grad_k, grad_v = unpack(grads)
    return attn_out, grad_q, grad_k, grad_v


def solution(mesh):
    placed = (P("ctx", "dp"), P(("ctx", "dp"), None), P(("ctx", "dp"), None), P("ctx", "dp"), P())
    return jax.shard_map(
        per_device,
        mesh=mesh,
        in_specs=placed,
        out_specs=(P("ctx", "dp"), P("ctx", "dp"), P(("ctx", "dp"), None), P(("ctx", "dp"), None)),
        check_vma=False,
    )
```

```python
import functools
import math

import jax
import jax.numpy as jnp
from jax import lax
from jax.experimental import pallas as pl
from jax.experimental.pallas import tpu as pltpu
from jax.sharding import PartitionSpec as P

HD = 128
TILE = 128
NEG = -1e30
F32 = jnp.float32
BF16 = jnp.bfloat16
SCALE = 1.0 / math.sqrt(HD)
LOG2_SCALE = SCALE * math.log2(math.e)


def dot_nt(a, b):
    return lax.dot_general(a, b, (((1,), (1,)), ((), ())), preferred_element_type=F32)


def dot_nn(a, b):
    return lax.dot_general(a, b, (((1,), (0,)), ((), ())), preferred_element_type=F32)


def by_rows(ref):
    return jnp.concatenate([ref[:, h * HD:(h + 1) * HD] for h in range(ref.shape[1] // HD)], axis=0)


def put_rows(ref, x):
    for h in range(ref.shape[1] // HD):
        ref[:, h * HD:(h + 1) * HD] = x[h * TILE:(h + 1) * TILE].astype(ref.dtype)


def write_bias(bias_ref, start_ref, first, count, offset, causal):
    startc = jnp.transpose(jnp.broadcast_to(start_ref[0], (TILE, TILE)))
    lane = lax.broadcasted_iota(jnp.int32, (TILE, TILE), 1)
    row = lax.broadcasted_iota(jnp.int32, (TILE, TILE), 0)
    for j in range(count):
        keep = lane >= startc - ((first + j) * TILE + offset)
        if causal and j == count - 1:
            keep = keep & (lane <= row)
        bias_ref[:, j * TILE:(j + 1) * TILE] = jnp.where(keep, 0.0, NEG)


def biased_scores(q, k, bias, heads):
    t = dot_nt(q, k) * LOG2_SCALE
    rows, width = t.shape
    return (t.reshape(heads, TILE, width) + bias[None]).reshape(rows, width)


def key_tiles(first_ref, i, tiles):
    first = lax.div(first_ref[i], TILE)
    return jnp.minimum(tiles + i - first, i) + 1, jnp.maximum(tiles - first, 0)


def local_forward(first_ref, start_ref, q_ref, g_ref, kv_ref, p_ref, o_ref, max_ref, out_ref, gs_ref, v_s, bias_s):
    i = pl.program_id(0)
    tiles = pl.num_programs(0)
    rows = kv_ref.shape[0]
    heads = q_ref.shape[1] // HD
    here, before = key_tiles(first_ref, i, tiles)

    @pl.when(i == 0)
    def _():
        v_s[:, :HD] = kv_ref[:, HD:]
        v_s[:, HD:] = jnp.ones((rows, HD), BF16)

    for w in range(1, rows // TILE + 1):
        @pl.when(here == w)
        def _(w=w):
            first = i - (w - 1)
            write_bias(bias_s, start_ref, first, w, rows, True)
            keys = pl.ds(pl.multiple_of(first * TILE, TILE), w * TILE)
            t = biased_scores(by_rows(q_ref), kv_ref[keys, :HD], bias_s[:, :w * TILE], heads)
            m = jnp.max(t, axis=1, keepdims=True)
            p = jnp.exp2(t - m).astype(BF16)
            p_ref[i, :, :w * TILE] = p
            o_ref[i] = dot_nn(p, v_s[keys, :])
            max_ref[i] = jnp.broadcast_to(m, max_ref.shape[1:])

    @pl.when(before == 0)
    def _():
        finish_rows(o_ref, g_ref, out_ref, gs_ref, i)


def finish_rows(o_ref, g_ref, out_ref, gs_ref, i):
    inv = 1.0 / o_ref[i, :, HD:]
    put_rows(out_ref, o_ref[i, :, :HD] * inv)
    put_rows(gs_ref, by_rows(g_ref).astype(F32) * inv)


def prev_step(first_ref, start_ref, q_ref, g_ref, kv_ref, o_ref, max_ref, out_any, gs_any,
              out_ref, gs_ref, dq_ref, dkv_ref, v_s, bias_s, dk_s, dv_s):
    i = pl.program_id(0)
    rows = kv_ref.shape[0]
    tiles = rows // TILE
    heads = q_ref.shape[1] // HD
    before = key_tiles(first_ref, i, tiles)[1]

    @pl.when(i == 0)
    def _():
        v_s[:, :HD] = kv_ref[:, HD:]
        v_s[:, HD:] = jnp.ones((rows, HD), BF16)
        dk_s[...] = jnp.zeros_like(dk_s)
        dv_s[...] = jnp.zeros_like(dv_s)

    @pl.when((i == 0) & (before == 0))
    def _():
        finish_rows(o_ref, g_ref, out_ref, gs_ref, 0)
        dq_ref[...] = jnp.zeros_like(dq_ref)

    for w in range(1, rows // TILE + 1):
        @pl.when(before == w)
        def _(w=w):
            first = rows // TILE - w
            write_bias(bias_s, start_ref, first, w, 0, False)
            keys = slice(first * TILE, rows)
            q = by_rows(q_ref)
            g = by_rows(g_ref).astype(F32)
            k = kv_ref[keys, :HD]
            t = biased_scores(q, k, bias_s[:, :w * TILE], heads)
            m1 = max_ref[i]
            m = jnp.maximum(m1, jnp.max(t, axis=1, keepdims=True))
            a1 = jnp.exp2(m1 - m)
            p = jnp.exp2(t - jnp.concatenate([m] * w, axis=1))
            pb = p.astype(BF16)
            o2 = dot_nn(pb, v_s[keys, :])
            inv = 1.0 / (a1 * o_ref[i, :, HD:] + o2[:, HD:])
            out = ((a1 * o_ref[i, :, :HD] + o2[:, :HD]) * inv).astype(BF16)
            g = g * inv
            gs = g.astype(BF16)
            put_rows(out_ref, out)
            put_rows(gs_ref, g * a1)
            delta = jnp.sum(gs.astype(F32) * out.astype(F32), axis=1, keepdims=True)
            ds = (p * (dot_nt(gs, kv_ref[keys, HD:]) - delta)).astype(BF16)
            put_rows(dq_ref, dot_nn(ds, k) * SCALE)
            add_grads(dk_s, dv_s, first, w, dot_nn(jnp.transpose(q), ds), dot_nn(jnp.transpose(gs), pb))

    @pl.when(i == pl.num_programs(0) - 1)
    def _():
        write_grads(dkv_ref, dk_s, dv_s)


def add_grads(dk_s, dv_s, first, count, dk, dv):
    for j in range(count):
        dk_s[first + j] += dk[:, j * TILE:(j + 1) * TILE]
        dv_s[first + j] += dv[:, j * TILE:(j + 1) * TILE]


def write_grads(ref, dk_s, dv_s):
    for j in range(dk_s.shape[0]):
        at = slice(j * TILE, (j + 1) * TILE)
        ref[at, :HD] = (jnp.transpose(dk_s[j]) * SCALE).astype(ref.dtype)
        ref[at, HD:] = jnp.transpose(dv_s[j]).astype(ref.dtype)


def local_backward(first_ref, q_ref, gs_ref, out_ref, p_ref, kv_ref, dq_ref, dkv_ref, dk_s, dv_s):
    i = pl.program_id(0)
    tiles = pl.num_programs(0)
    rows = kv_ref.shape[0]
    here = key_tiles(first_ref, i, tiles)[0]

    @pl.when(i == 0)
    def _():
        dk_s[...] = jnp.zeros_like(dk_s)
        dv_s[...] = jnp.zeros_like(dv_s)

    for w in range(1, rows // TILE + 1):
        @pl.when(here == w)
        def _(w=w):
            first = i - (w - 1)
            keys = pl.ds(pl.multiple_of(first * TILE, TILE), w * TILE)
            q = by_rows(q_ref)
            gs = by_rows(gs_ref)
            pb = p_ref[i, :, :w * TILE]
            delta = jnp.sum(gs.astype(F32) * by_rows(out_ref).astype(F32), axis=1, keepdims=True)
            ds = (pb.astype(F32) * (dot_nt(gs, kv_ref[keys, HD:]) - delta)).astype(BF16)
            put_rows(dq_ref, dot_nn(ds, kv_ref[keys, :HD]) * SCALE)
            add_grads(dk_s, dv_s, first, w, dot_nn(jnp.transpose(q), ds), dot_nn(jnp.transpose(gs), pb))

    @pl.when(i == tiles - 1)
    def _():
        write_grads(dkv_ref, dk_s, dv_s)


def call(body, name, rows, steps, ins, outs, scratch, flops, limit, aliases={}):
    big = rows * 4 * HD

    def in_hbm(x):
        if isinstance(x, jax.ShapeDtypeStruct) and math.prod(x.shape) >= big:
            return pltpu.HBM(x.shape, x.dtype)
        return x

    run = pl.pallas_call(
        body,
        grid_spec=pltpu.PrefetchScalarGridSpec(
            num_scalar_prefetch=1, grid=(steps,), in_specs=ins, out_specs=[s for s, _ in outs], scratch_shapes=scratch
        ),
        out_shape=[in_hbm(s) for _, s in outs],
        input_output_aliases=aliases,
        compiler_params=pltpu.CompilerParams(dimension_semantics=("arbitrary",), vmem_limit_bytes=limit << 20),
        cost_estimate=pl.CostEstimate(flops=flops, transcendentals=0, bytes_accessed=8 << 20),
        name=name,
    )
    return lambda n, *args: run(n, *[pltpu.with_memory_space_constraint(x, pltpu.HBM) if x.ndim == 2 and x.size >= big else x for x in args])


def attention_calls(first, starts, q, g):
    rows, width = q.shape
    tiles = rows // TILE
    sds = jax.ShapeDtypeStruct
    own_tile = lambda i, n: i
    met_tile = lambda i, n: n[tiles + i]
    whole = pl.BlockSpec((rows, 2 * HD), lambda i, n: (0, 0))

    def flat(at, w=width):
        return pl.BlockSpec((TILE, w), lambda i, n: (at(i, n), 0))

    def slab(at, *dims):
        return pl.BlockSpec((1,) + dims, lambda i, n: (at(i, n), 0, 0))

    held = pl.BlockSpec(memory_space=pltpu.VMEM)
    there = pl.BlockSpec(memory_space=pl.ANY)
    grads = [pltpu.VMEM((tiles, HD, TILE), F32)] * 2
    shared = [pltpu.VMEM((rows, 2 * HD), BF16), pltpu.VMEM((TILE, rows), F32)]
    rows_bf16 = sds((rows, width), BF16)

    def forward_local(own):
        return call(
            local_forward, "local_forward", rows, tiles,
            [slab(own_tile, 1, TILE), flat(own_tile), flat(own_tile), whole],
            [
                (held, pltpu.VMEM((tiles, width, rows), BF16)),
                (held, pltpu.VMEM((tiles, width, 2 * HD), F32)),
                (held, pltpu.VMEM((tiles, width, HD), F32)),
                (flat(own_tile), rows_bf16),
                (flat(own_tile), rows_bf16),
            ],
            shared, 3 << 30, 28,
        )(first, starts, q, g, own)

    def finish_prev(prev, o, maxes, out, gs):
        return call(
            prev_step, "previous_block", rows, tiles,
            [
                slab(met_tile, 1, TILE), flat(met_tile), flat(met_tile), whole,
                held, held, there, there,
            ],
            [
                (flat(met_tile), rows_bf16), (flat(met_tile), rows_bf16), (flat(met_tile), rows_bf16),
                (whole, sds((rows, 2 * HD), BF16)),
            ],
            shared + grads, 4 << 30, 28, {7: 0, 8: 1},
        )(first, starts, q, g, prev, o, maxes, out, gs)

    def backward_local(gs, out, p, own):
        return call(
            local_backward, "local_backward", rows, tiles,
            [flat(own_tile), flat(own_tile), flat(own_tile), held, whole],
            [(flat(own_tile), rows_bf16), (whole, sds((rows, 2 * HD), F32))],
            grads, 5 << 30, 28,
        )(first, q, gs, out, p, own)

    return forward_local, finish_prev, backward_local


def pack_kernel(k_ref, v_ref, out_ref, sems):
    copies = []
    for h in range(out_ref.shape[0]):
        at = pl.ds(h * HD, HD)
        copies.append(pltpu.make_async_copy(k_ref.at[:, at], out_ref.at[h, :, pl.ds(0, HD)], sems.at[0, h]))
        copies.append(pltpu.make_async_copy(v_ref.at[:, at], out_ref.at[h, :, pl.ds(HD, HD)], sems.at[1, h]))
    for copy in copies:
        copy.start()
    for copy in copies:
        copy.wait()


def unpack_kernel(x_ref, k_ref, v_ref):
    for h in range(x_ref.shape[0]):
        k_ref[:, h * HD:(h + 1) * HD] = x_ref[h, :, :HD]
        v_ref[:, h * HD:(h + 1) * HD] = x_ref[h, :, HD:]


def pack(keys, values):
    tokens, width = keys.shape
    heads = width // HD
    return pl.pallas_call(
        pack_kernel,
        in_specs=[pl.BlockSpec(memory_space=pl.ANY)] * 2,
        out_specs=pl.BlockSpec(memory_space=pl.ANY),
        scratch_shapes=[pltpu.SemaphoreType.DMA((2, heads))],
        out_shape=jax.ShapeDtypeStruct((heads, tokens, 2 * HD), BF16),
        name="pack_heads",
    )(keys, values)


def unpack(x):
    heads, tokens, _ = x.shape
    return pl.pallas_call(
        unpack_kernel,
        in_specs=[pl.BlockSpec(memory_space=pltpu.VMEM)],
        out_shape=[jax.ShapeDtypeStruct((tokens, heads * HD), BF16)] * 2,
        name="unpack_heads",
    )(pltpu.with_memory_space_constraint(x, pltpu.VMEM))


def passed_along(x, axis, by, ring):
    count = lax.axis_size(axis)
    pairs = [(i, (i + by) % count) for i in range(count) if ring or 0 <= i + by < count]
    return lax.ppermute(x, axis, pairs)


def per_device(queries, keys, values, grad_out, doc_lengths):
    rows = queries.shape[0]
    shared = pack(keys, values)
    own = lax.all_to_all(shared, "dp", split_axis=0, concat_axis=0, tiled=True).reshape(rows, 2 * HD)
    first_pos = lax.axis_index("ctx") * rows
    ends = jnp.cumsum(doc_lengths)
    positions = first_pos + jnp.arange(rows, dtype=jnp.int32)
    starts = jnp.max(jnp.where(ends[None, :] <= positions[:, None], ends[None, :], 0), axis=1)
    starts = (starts - first_pos + rows).astype(jnp.int32)
    tiles = rows // TILE
    first = starts[::TILE]
    crossing = jnp.sum(first < rows, dtype=jnp.int32)
    met = jnp.minimum(jnp.arange(tiles, dtype=jnp.int32), jnp.maximum(crossing - 1, 0))
    first = jnp.concatenate([first, met])
    own, first = lax.optimization_barrier((own, first))
    prev = passed_along(own, "ctx", 1, True)
    forward_local, finish_prev, backward_local = attention_calls(
        first, starts.reshape(tiles, 1, TILE), queries, grad_out
    )
    probs, sums, maxes, out, scaled = forward_local(own)
    attn_out, scaled, grad_q_prev, back = finish_prev(prev, sums, maxes, out, scaled)
    grad_q, mine = backward_local(scaled, attn_out, probs, own)
    total = (mine + passed_along(back, "ctx", -1, False).astype(F32)).astype(BF16)
    total = total.reshape(shared.shape)
    grads = lax.all_to_all(total, "dp", split_axis=0, concat_axis=0, tiled=True)
    met_rows = lax.broadcasted_iota(jnp.int32, (rows, 1), 0) < crossing * TILE
    grad_q = (grad_q.astype(F32) + jnp.where(met_rows, grad_q_prev.astype(F32), 0.0)).astype(BF16)
    grad_k, grad_v = unpack(grads)
    return attn_out, grad_q, grad_k, grad_v


def solution(mesh):
    placed = (P("ctx", "dp"), P(("ctx", "dp"), None), P(("ctx", "dp"), None), P("ctx", "dp"), P())
    return jax.shard_map(
        per_device,
        mesh=mesh,
        in_specs=placed,
        out_specs=(P("ctx", "dp"), P("ctx", "dp"), P(("ctx", "dp"), None), P(("ctx", "dp"), None)),
        check_vma=False,
    )
```

```python
import functools
import math

import jax
import jax.numpy as jnp
from jax import lax
from jax.experimental import pallas as pl
from jax.experimental.pallas import tpu as pltpu
from jax.sharding import PartitionSpec as P

HD = 128
TILE = 128
NEG = -1e30
F32 = jnp.float32
BF16 = jnp.bfloat16
SCALE = 1.0 / math.sqrt(HD)
LOG2_SCALE = SCALE * math.log2(math.e)


def dot_nt(a, b):
    return lax.dot_general(a, b, (((1,), (1,)), ((), ())), preferred_element_type=F32)


def dot_nn(a, b):
    return lax.dot_general(a, b, (((1,), (0,)), ((), ())), preferred_element_type=F32)


def by_rows(ref, heads=None):
    heads = range(ref.shape[1] // HD) if heads is None else heads
    return jnp.concatenate([ref[:, h * HD:(h + 1) * HD] for h in heads], axis=0)


def put_rows(ref, x, heads=None):
    heads = range(ref.shape[1] // HD) if heads is None else heads
    for j, h in enumerate(heads):
        ref[:, h * HD:(h + 1) * HD] = x[j * TILE:(j + 1) * TILE].astype(ref.dtype)


def head_groups(heads, count):
    size = heads // count
    return [(range(j * size, (j + 1) * size), slice(j * size * TILE, (j + 1) * size * TILE)) for j in range(count)]


def write_bias(bias_ref, start_ref, first, count, offset, causal):
    startc = jnp.transpose(jnp.broadcast_to(start_ref[0], (TILE, TILE)))
    lane = lax.broadcasted_iota(jnp.int32, (TILE, TILE), 1)
    row = lax.broadcasted_iota(jnp.int32, (TILE, TILE), 0)
    for j in range(count):
        keep = lane >= startc - ((first + j) * TILE + offset)
        if causal and j == count - 1:
            keep = keep & (lane <= row)
        bias_ref[:, j * TILE:(j + 1) * TILE] = jnp.where(keep, 0.0, NEG)


def biased_scores(q, k, bias, heads):
    t = dot_nt(q, k) * LOG2_SCALE
    rows, width = t.shape
    return (t.reshape(heads, TILE, width) + bias[None]).reshape(rows, width)


def key_tiles(first_ref, i, tiles):
    first = lax.div(first_ref[i], TILE)
    return jnp.minimum(tiles + i - first, i) + 1, jnp.maximum(tiles - first, 0)


def local_forward(first_ref, start_ref, q_ref, g_ref, kv_ref, p_ref, o_ref, max_ref, out_ref, gs_ref, v_s, bias_s):
    i = pl.program_id(0)
    tiles = pl.num_programs(0)
    rows = kv_ref.shape[0]
    heads = q_ref.shape[1] // HD
    here, before = key_tiles(first_ref, i, tiles)

    @pl.when(i == 0)
    def _():
        v_s[:, :HD] = kv_ref[:, HD:]
        v_s[:, HD:] = jnp.ones((rows, HD), BF16)

    for w in range(1, rows // TILE + 1):
        @pl.when(here == w)
        def _(w=w):
            first = i - (w - 1)
            write_bias(bias_s, start_ref, first, w, rows, True)
            keys = pl.ds(pl.multiple_of(first * TILE, TILE), w * TILE)
            for hs, at in head_groups(heads, 2 if w > 3 else 1):
                t = biased_scores(by_rows(q_ref, hs), kv_ref[keys, :HD], bias_s[:, :w * TILE], len(hs))
                m = jnp.max(t, axis=1, keepdims=True)
                p = jnp.exp2(t - m).astype(BF16)
                p_ref[i, at, :w * TILE] = p
                o_ref[i, at] = dot_nn(p, v_s[keys, :])
                max_ref[i, at] = jnp.broadcast_to(m, (m.shape[0], HD))

    @pl.when(before == 0)
    def _():
        finish_rows(o_ref, g_ref, out_ref, gs_ref, i)


def finish_rows(o_ref, g_ref, out_ref, gs_ref, i):
    inv = 1.0 / o_ref[i, :, HD:]
    put_rows(out_ref, o_ref[i, :, :HD] * inv)
    put_rows(gs_ref, by_rows(g_ref).astype(F32) * inv)


def prev_step(first_ref, start_ref, q_ref, g_ref, kv_ref, o_ref, max_ref, out_any, gs_any,
              out_ref, gs_ref, ds_ref, dkv_ref, v_s, bias_s, dk_s, dv_s):
    i = pl.program_id(0)
    rows = kv_ref.shape[0]
    tiles = rows // TILE
    heads = q_ref.shape[1] // HD
    before = key_tiles(first_ref, i, tiles)[1]

    @pl.when(i == 0)
    def _():
        v_s[:, :HD] = kv_ref[:, HD:]
        v_s[:, HD:] = jnp.ones((rows, HD), BF16)
        dk_s[...] = jnp.zeros_like(dk_s)
        dv_s[...] = jnp.zeros_like(dv_s)

    @pl.when((i == 0) & (before == 0))
    def _():
        finish_rows(o_ref, g_ref, out_ref, gs_ref, 0)

    for w in range(1, rows // TILE + 1):
        @pl.when(before == w)
        def _(w=w):
            first = rows // TILE - w
            write_bias(bias_s, start_ref, first, w, 0, False)
            keys = slice(first * TILE, rows)
            for hs, at in head_groups(heads, 1):
                q = by_rows(q_ref, hs)
                g = by_rows(g_ref, hs).astype(F32)
                t = biased_scores(q, kv_ref[keys, :HD], bias_s[:, :w * TILE], len(hs))
                m1 = max_ref[i, at]
                m = jnp.maximum(m1, jnp.max(t, axis=1, keepdims=True))
                a1 = jnp.exp2(m1 - m)
                p = jnp.exp2(t - jnp.concatenate([m] * w, axis=1))
                pb = p.astype(BF16)
                o2 = dot_nn(pb, v_s[keys, :])
                inv = 1.0 / (a1 * o_ref[i, at, HD:] + o2[:, HD:])
                out = ((a1 * o_ref[i, at, :HD] + o2[:, :HD]) * inv).astype(BF16)
                g = g * inv
                gs = g.astype(BF16)
                put_rows(out_ref, out, hs)
                put_rows(gs_ref, g * a1, hs)
                delta = jnp.sum(gs.astype(F32) * out.astype(F32), axis=1, keepdims=True)
                ds = (p * (dot_nt(gs, kv_ref[keys, HD:]) - delta)).astype(BF16)
                ds_ref[i, at, :w * TILE] = ds
                add_grads(dk_s, dv_s, first, w, dot_nn(jnp.transpose(q), ds), dot_nn(jnp.transpose(gs), pb))

    @pl.when(i == pl.num_programs(0) - 1)
    def _():
        write_grads(dkv_ref, dk_s, dv_s, key_tiles(first_ref, 0, tiles)[1])


def add_grads(dk_s, dv_s, first, count, dk, dv):
    for j in range(count):
        dk_s[first + j] += dk[:, j * TILE:(j + 1) * TILE]
        dv_s[first + j] += dv[:, j * TILE:(j + 1) * TILE]


def write_grads(ref, dk_s, dv_s, count):
    tiles = dk_s.shape[0]
    for j in range(tiles):
        at = slice(j * TILE, (j + 1) * TILE)

        @pl.when(j >= tiles - count)
        def _(j=j, at=at):
            ref[at, :HD] = (jnp.transpose(dk_s[j]) * SCALE).astype(ref.dtype)
            ref[at, HD:] = jnp.transpose(dv_s[j]).astype(ref.dtype)

        @pl.when(j < tiles - count)
        def _(at=at):
            ref[at, :] = jnp.zeros((TILE, 2 * HD), ref.dtype)


def local_backward(first_ref, q_ref, gs_ref, out_ref, p_ref, dsp_ref, kvp_ref, kv_ref, dq_ref, dkv_ref, dk_s, dv_s):
    i = pl.program_id(0)
    tiles = pl.num_programs(0)
    rows = kv_ref.shape[0]
    here, before = key_tiles(first_ref, i, tiles)

    @pl.when(i == 0)
    def _():
        dk_s[...] = jnp.zeros_like(dk_s)
        dv_s[...] = jnp.zeros_like(dv_s)

    for w in range(1, rows // TILE + 1):
        @pl.when(here == w)
        def _(w=w):
            first = i - (w - 1)
            keys = pl.ds(pl.multiple_of(first * TILE, TILE), w * TILE)
            for hs, at in head_groups(q_ref.shape[1] // HD, 1):
                q = by_rows(q_ref, hs)
                gs = by_rows(gs_ref, hs)
                pb = p_ref[i, at, :w * TILE]
                delta = jnp.sum(gs.astype(F32) * by_rows(out_ref, hs).astype(F32), axis=1, keepdims=True)
                ds = (pb.astype(F32) * (dot_nt(gs, kv_ref[keys, HD:]) - delta)).astype(BF16)
                put_rows(dq_ref, dot_nn(ds, kv_ref[keys, :HD]) * SCALE, hs)
                add_grads(dk_s, dv_s, first, w, dot_nn(jnp.transpose(q), ds), dot_nn(jnp.transpose(gs), pb))

    for w in range(1, rows // TILE + 1):
        @pl.when(before == w)
        def _(w=w):
            dq = dot_nn(dsp_ref[i, :, :w * TILE], kvp_ref[rows - w * TILE:, :HD]) * SCALE
            put_rows(dq_ref, by_rows(dq_ref).astype(F32) + dq)

    @pl.when(i == tiles - 1)
    def _():
        write_grads(dkv_ref, dk_s, dv_s, tiles)


def call(body, name, rows, steps, ins, outs, scratch, flops, limit, aliases={}):
    big = rows * 4 * HD

    def in_hbm(x):
        if isinstance(x, jax.ShapeDtypeStruct) and math.prod(x.shape) >= big:
            return pltpu.HBM(x.shape, x.dtype)
        return x

    run = pl.pallas_call(
        body,
        grid_spec=pltpu.PrefetchScalarGridSpec(
            num_scalar_prefetch=1, grid=(steps,), in_specs=ins, out_specs=[s for s, _ in outs], scratch_shapes=scratch
        ),
        out_shape=[in_hbm(s) for _, s in outs],
        input_output_aliases=aliases,
        compiler_params=pltpu.CompilerParams(dimension_semantics=("arbitrary",), vmem_limit_bytes=limit << 20),
        cost_estimate=pl.CostEstimate(flops=flops, transcendentals=0, bytes_accessed=8 << 20),
        name=name,
    )
    return lambda n, *args: run(n, *[pltpu.with_memory_space_constraint(x, pltpu.HBM) if x.ndim == 2 and x.size >= big else x for x in args])


def attention_calls(first, starts, q, g):
    rows, width = q.shape
    tiles = rows // TILE
    sds = jax.ShapeDtypeStruct
    own_tile = lambda i, n: i
    met_tile = lambda i, n: n[tiles + i]
    whole = pl.BlockSpec((rows, 2 * HD), lambda i, n: (0, 0))

    def flat(at, w=width):
        return pl.BlockSpec((TILE, w), lambda i, n: (at(i, n), 0))

    def slab(at, *dims):
        return pl.BlockSpec((1,) + dims, lambda i, n: (at(i, n), 0, 0))

    held = pl.BlockSpec(memory_space=pltpu.VMEM)
    there = pl.BlockSpec(memory_space=pl.ANY)
    grads = [pltpu.VMEM((tiles, HD, TILE), F32)] * 2
    shared = [pltpu.VMEM((rows, 2 * HD), BF16), pltpu.VMEM((TILE, rows), F32)]
    rows_bf16 = sds((rows, width), BF16)

    def forward_local(own):
        return call(
            local_forward, "local_forward", rows, tiles,
            [slab(own_tile, 1, TILE), flat(own_tile), flat(own_tile), whole],
            [
                (held, pltpu.VMEM((tiles, width, rows), BF16)),
                (held, pltpu.VMEM((tiles, width, 2 * HD), F32)),
                (held, pltpu.VMEM((tiles, width, HD), F32)),
                (flat(own_tile), rows_bf16),
                (flat(own_tile), rows_bf16),
            ],
            shared, 3 << 30, 24,
        )(first, starts, q, g, own)

    def finish_prev(prev, o, maxes, out, gs):
        return call(
            prev_step, "previous_block", rows, tiles,
            [
                slab(met_tile, 1, TILE), flat(met_tile), flat(met_tile), whole,
                held, held, there, there,
            ],
            [
                (flat(met_tile), rows_bf16), (flat(met_tile), rows_bf16),
                (held, pltpu.VMEM((tiles, width, rows), BF16)), (whole, sds((rows, 2 * HD), BF16)),
            ],
            shared + grads, 4 << 30, 24, {7: 0, 8: 1},
        )(first, starts, q, g, prev, o, maxes, out, gs)

    def backward_local(gs, out, p, dsp, prev, own):
        return call(
            local_backward, "local_backward", rows, tiles,
            [flat(own_tile), flat(own_tile), flat(own_tile), held, held, whole, whole],
            [(flat(own_tile), rows_bf16), (whole, sds((rows, 2 * HD), F32))],
            grads, 5 << 30, 24,
        )(first, q, gs, out, p, dsp, prev, own)

    return forward_local, finish_prev, backward_local


def pack_kernel(k_ref, v_ref, out_ref):
    for h in range(out_ref.shape[0]):
        out_ref[h, :, :HD] = k_ref[:, h * HD:(h + 1) * HD]
        out_ref[h, :, HD:] = v_ref[:, h * HD:(h + 1) * HD]


def unpack_kernel(x_ref, k_ref, v_ref):
    for h in range(x_ref.shape[0]):
        k_ref[:, h * HD:(h + 1) * HD] = x_ref[h, :, :HD]
        v_ref[:, h * HD:(h + 1) * HD] = x_ref[h, :, HD:]


def pack(keys, values):
    tokens, width = keys.shape
    heads = width // HD
    half = pl.BlockSpec((tokens, width // 2), lambda i: (0, i))
    return pl.pallas_call(
        pack_kernel,
        grid=(2,),
        in_specs=[half, half],
        out_specs=pl.BlockSpec((heads // 2, tokens, 2 * HD), lambda i: (i, 0, 0)),
        out_shape=jax.ShapeDtypeStruct((heads, tokens, 2 * HD), BF16),
        name="pack_heads",
    )(keys, values)


def unpack(x):
    heads, tokens, _ = x.shape
    return pl.pallas_call(
        unpack_kernel,
        in_specs=[pl.BlockSpec(memory_space=pltpu.VMEM)],
        out_shape=[jax.ShapeDtypeStruct((tokens, heads * HD), BF16)] * 2,
        name="unpack_heads",
    )(pltpu.with_memory_space_constraint(x, pltpu.VMEM))


def passed_along(x, axis, by, ring):
    count = lax.axis_size(axis)
    pairs = [(i, (i + by) % count) for i in range(count) if ring or 0 <= i + by < count]
    return lax.ppermute(x, axis, pairs)


def per_device(queries, keys, values, grad_out, doc_lengths):
    rows = queries.shape[0]
    shared = pack(keys, values)
    own = lax.all_to_all(shared, "dp", split_axis=0, concat_axis=0, tiled=True).reshape(rows, 2 * HD)
    first_pos = lax.axis_index("ctx") * rows
    ends = jnp.cumsum(doc_lengths)
    positions = first_pos + jnp.arange(rows, dtype=jnp.int32)
    starts = jnp.max(jnp.where(ends[None, :] <= positions[:, None], ends[None, :], 0), axis=1)
    starts = (starts - first_pos + rows).astype(jnp.int32)
    tiles = rows // TILE
    first = starts[::TILE]
    crossing = jnp.sum(first < rows, dtype=jnp.int32)
    met = jnp.minimum(jnp.arange(tiles, dtype=jnp.int32), jnp.maximum(crossing - 1, 0))
    first = jnp.concatenate([first, met])
    own, first = lax.optimization_barrier((own, first))
    prev = passed_along(own, "ctx", 1, True)
    forward_local, finish_prev, backward_local = attention_calls(
        first, starts.reshape(tiles, 1, TILE), queries, grad_out
    )
    probs, sums, maxes, out, scaled = forward_local(own)
    attn_out, scaled, grad_scores, back = finish_prev(prev, sums, maxes, out, scaled)
    grad_q, mine = backward_local(scaled, attn_out, probs, grad_scores, prev, own)
    total = (mine + passed_along(back, "ctx", -1, False).astype(F32)).astype(BF16)
    total = total.reshape(shared.shape)
    grads = lax.all_to_all(total, "dp", split_axis=0, concat_axis=0, tiled=True)
    grad_k, grad_v = unpack(grads)
    return attn_out, grad_q, grad_k, grad_v


def solution(mesh):
    placed = (P("ctx", "dp"), P(("ctx", "dp"), None), P(("ctx", "dp"), None), P("ctx", "dp"), P())
    return jax.shard_map(
        per_device,
        mesh=mesh,
        in_specs=placed,
        out_specs=(P("ctx", "dp"), P("ctx", "dp"), P(("ctx", "dp"), None), P(("ctx", "dp"), None)),
        check_vma=False,
    )
```

```python
import functools
import math

import jax
import jax.numpy as jnp
from jax import lax
from jax.experimental import pallas as pl
from jax.experimental.pallas import tpu as pltpu
from jax.sharding import PartitionSpec as P

HD = 128
TILE = 128
NEG = -1e30
F32 = jnp.float32
BF16 = jnp.bfloat16
SCALE = 1.0 / math.sqrt(HD)
LOG2_SCALE = SCALE * math.log2(math.e)


def dot_nt(a, b):
    return lax.dot_general(a, b, (((1,), (1,)), ((), ())), preferred_element_type=F32)


def dot_nn(a, b):
    return lax.dot_general(a, b, (((1,), (0,)), ((), ())), preferred_element_type=F32)


def by_rows(ref, heads=None):
    heads = range(ref.shape[1] // HD) if heads is None else heads
    return jnp.concatenate([ref[:, h * HD:(h + 1) * HD] for h in heads], axis=0)


def put_rows(ref, x, heads=None):
    heads = range(ref.shape[1] // HD) if heads is None else heads
    for j, h in enumerate(heads):
        ref[:, h * HD:(h + 1) * HD] = x[j * TILE:(j + 1) * TILE].astype(ref.dtype)


def head_groups(heads, count):
    size = heads // count
    return [(range(j * size, (j + 1) * size), slice(j * size * TILE, (j + 1) * size * TILE)) for j in range(count)]


def write_bias(bias_ref, start_ref, first, count, offset, causal):
    startc = jnp.transpose(jnp.broadcast_to(start_ref[0], (TILE, TILE)))
    lane = lax.broadcasted_iota(jnp.int32, (TILE, TILE), 1)
    row = lax.broadcasted_iota(jnp.int32, (TILE, TILE), 0)
    for j in range(count):
        keep = lane >= startc - ((first + j) * TILE + offset)
        if causal and j == count - 1:
            keep = keep & (lane <= row)
        bias_ref[:, j * TILE:(j + 1) * TILE] = jnp.where(keep, 0.0, NEG)


def biased_scores(q, k, bias, heads):
    t = dot_nt(q, k) * LOG2_SCALE
    rows, width = t.shape
    return (t.reshape(heads, TILE, width) + bias[None]).reshape(rows, width)


def key_tiles(first_ref, i, tiles):
    first = lax.div(first_ref[i], TILE)
    return jnp.minimum(tiles + i - first, i) + 1, jnp.maximum(tiles - first, 0)


def local_forward(first_ref, start_ref, q_ref, g_ref, kv_ref, p_ref, o_ref, max_ref, out_ref, gs_ref, v_s, bias_s):
    i = pl.program_id(0)
    tiles = pl.num_programs(0)
    rows = kv_ref.shape[0]
    heads = q_ref.shape[1] // HD
    here, before = key_tiles(first_ref, i, tiles)

    @pl.when(i == 0)
    def _():
        v_s[:, :HD] = kv_ref[:, HD:]
        v_s[:, HD:] = jnp.ones((rows, HD), BF16)

    for w in range(1, rows // TILE + 1):
        @pl.when(here == w)
        def _(w=w):
            first = i - (w - 1)
            write_bias(bias_s, start_ref, first, w, rows, True)
            keys = pl.ds(pl.multiple_of(first * TILE, TILE), w * TILE)
            for hs, at in head_groups(heads, 2 if w > 3 else 1):
                t = biased_scores(by_rows(q_ref, hs), kv_ref[keys, :HD], bias_s[:, :w * TILE], len(hs))
                m = jnp.max(t, axis=1, keepdims=True)
                p = jnp.exp2(t - m).astype(BF16)
                p_ref[i, at, :w * TILE] = p
                o_ref[i, at] = dot_nn(p, v_s[keys, :])
                max_ref[i, at] = jnp.broadcast_to(m, (m.shape[0], HD))

    @pl.when(before == 0)
    def _():
        finish_rows(o_ref, g_ref, out_ref, gs_ref, i)


def finish_rows(o_ref, g_ref, out_ref, gs_ref, i):
    inv = 1.0 / o_ref[i, :, HD:]
    put_rows(out_ref, o_ref[i, :, :HD] * inv)
    put_rows(gs_ref, by_rows(g_ref).astype(F32) * inv)


def prev_step(first_ref, start_ref, q_ref, g_ref, kv_ref, o_ref, max_ref, out_any, gs_any,
              out_ref, gs_ref, ds_ref, dkv_ref, v_s, bias_s, dk_s, dv_s):
    i = pl.program_id(0)
    rows = kv_ref.shape[0]
    tiles = rows // TILE
    heads = q_ref.shape[1] // HD
    before = key_tiles(first_ref, i, tiles)[1]

    @pl.when(i == 0)
    def _():
        v_s[:, :HD] = kv_ref[:, HD:]
        v_s[:, HD:] = jnp.ones((rows, HD), BF16)
        dk_s[...] = jnp.zeros_like(dk_s)
        dv_s[...] = jnp.zeros_like(dv_s)

    @pl.when((i == 0) & (before == 0))
    def _():
        finish_rows(o_ref, g_ref, out_ref, gs_ref, 0)

    for w in range(1, rows // TILE + 1):
        @pl.when(before == w)
        def _(w=w):
            first = rows // TILE - w
            write_bias(bias_s, start_ref, first, w, 0, False)
            keys = slice(first * TILE, rows)
            for hs, at in head_groups(heads, 1):
                q = by_rows(q_ref, hs)
                g = by_rows(g_ref, hs).astype(F32)
                t = biased_scores(q, kv_ref[keys, :HD], bias_s[:, :w * TILE], len(hs))
                m1 = max_ref[i, at]
                m = jnp.maximum(m1, jnp.max(t, axis=1, keepdims=True))
                a1 = jnp.exp2(m1 - m)
                p = jnp.exp2(t - jnp.concatenate([m] * w, axis=1))
                pb = p.astype(BF16)
                o2 = dot_nn(pb, v_s[keys, :])
                inv = 1.0 / (a1 * o_ref[i, at, HD:] + o2[:, HD:])
                out = ((a1 * o_ref[i, at, :HD] + o2[:, :HD]) * inv).astype(BF16)
                g = g * inv
                gs = g.astype(BF16)
                put_rows(out_ref, out, hs)
                put_rows(gs_ref, g * a1, hs)
                delta = jnp.sum(gs.astype(F32) * out.astype(F32), axis=1, keepdims=True)
                ds = (p * (dot_nt(gs, kv_ref[keys, HD:]) - delta)).astype(BF16)
                ds_ref[i, at, :w * TILE] = ds
                add_grads(dk_s, dv_s, first, w, dot_nn(jnp.transpose(q), ds), dot_nn(jnp.transpose(gs), pb))

    @pl.when(i == pl.num_programs(0) - 1)
    def _():
        write_grads(dkv_ref, dk_s, dv_s, key_tiles(first_ref, 0, tiles)[1])


def add_grads(dk_s, dv_s, first, count, dk, dv):
    for j in range(count):
        dk_s[first + j] += dk[:, j * TILE:(j + 1) * TILE]
        dv_s[first + j] += dv[:, j * TILE:(j + 1) * TILE]


def write_grads(ref, dk_s, dv_s, count):
    tiles = dk_s.shape[0]
    for j in range(tiles):
        at = slice(j * TILE, (j + 1) * TILE)

        @pl.when(j >= tiles - count)
        def _(j=j, at=at):
            ref[at, :HD] = (jnp.transpose(dk_s[j]) * SCALE).astype(ref.dtype)
            ref[at, HD:] = jnp.transpose(dv_s[j]).astype(ref.dtype)

        @pl.when(j < tiles - count)
        def _(at=at):
            ref[at, :] = jnp.zeros((TILE, 2 * HD), ref.dtype)


def local_backward(first_ref, q_ref, gs_ref, out_ref, p_ref, dsp_ref, kvp_ref, kv_ref, dq_ref, dkv_ref, dk_s, dv_s):
    i = pl.program_id(0)
    tiles = pl.num_programs(0)
    rows = kv_ref.shape[0]
    here, before = key_tiles(first_ref, i, tiles)

    @pl.when(i == 0)
    def _():
        dk_s[...] = jnp.zeros_like(dk_s)
        dv_s[...] = jnp.zeros_like(dv_s)

    for w in range(1, rows // TILE + 1):
        @pl.when(here == w)
        def _(w=w):
            first = i - (w - 1)
            keys = pl.ds(pl.multiple_of(first * TILE, TILE), w * TILE)
            for hs, at in head_groups(q_ref.shape[1] // HD, 1):
                q = by_rows(q_ref, hs)
                gs = by_rows(gs_ref, hs)
                pb = p_ref[i, at, :w * TILE]
                delta = jnp.sum(gs.astype(F32) * by_rows(out_ref, hs).astype(F32), axis=1, keepdims=True)
                ds = (pb.astype(F32) * (dot_nt(gs, kv_ref[keys, HD:]) - delta)).astype(BF16)
                put_rows(dq_ref, dot_nn(ds, kv_ref[keys, :HD]) * SCALE, hs)
                add_grads(dk_s, dv_s, first, w, dot_nn(jnp.transpose(q), ds), dot_nn(jnp.transpose(gs), pb))

    for w in range(1, rows // TILE + 1):
        @pl.when(before == w)
        def _(w=w):
            dq = dot_nn(dsp_ref[i, :, :w * TILE], kvp_ref[rows - w * TILE:, :HD]) * SCALE
            put_rows(dq_ref, by_rows(dq_ref).astype(F32) + dq)

    @pl.when(i == tiles - 1)
    def _():
        write_grads(dkv_ref, dk_s, dv_s, tiles)


def call(body, name, rows, steps, ins, outs, scratch, flops, limit, aliases={}):
    big = rows * 4 * HD

    def placed(x):
        if isinstance(x, jax.ShapeDtypeStruct) and math.prod(x.shape) >= big:
            return pltpu.HBM(x.shape, x.dtype)
        return x

    run = pl.pallas_call(
        body,
        grid_spec=pltpu.PrefetchScalarGridSpec(
            num_scalar_prefetch=1, grid=(steps,), in_specs=ins, out_specs=[s for s, _ in outs], scratch_shapes=scratch
        ),
        out_shape=[placed(s) for _, s in outs],
        input_output_aliases=aliases,
        compiler_params=pltpu.CompilerParams(dimension_semantics=("arbitrary",), vmem_limit_bytes=limit << 20),
        cost_estimate=pl.CostEstimate(flops=flops, transcendentals=0, bytes_accessed=8 << 20),
        name=name,
    )
    return run


def in_hbm(x):
    return pltpu.with_memory_space_constraint(x, pltpu.HBM)


def attention_calls(first, starts, q, g):
    rows, width = q.shape
    tiles = rows // TILE
    q = pltpu.with_memory_space_constraint(q, pltpu.VMEM)
    g_near = pltpu.with_memory_space_constraint(g, pltpu.VMEM)
    sds = jax.ShapeDtypeStruct
    own_tile = lambda i, n: i
    met_tile = lambda i, n: n[tiles + i]
    whole = pl.BlockSpec((rows, 2 * HD), lambda i, n: (0, 0))

    def flat(at, w=width):
        return pl.BlockSpec((TILE, w), lambda i, n: (at(i, n), 0))

    def slab(at, *dims):
        return pl.BlockSpec((1,) + dims, lambda i, n: (at(i, n), 0, 0))

    held = pl.BlockSpec(memory_space=pltpu.VMEM)
    there = pl.BlockSpec(memory_space=pl.ANY)
    grads = [pltpu.VMEM((tiles, HD, TILE), F32)] * 2
    shared = [pltpu.VMEM((rows, 2 * HD), BF16), pltpu.VMEM((TILE, rows), F32)]
    rows_bf16 = sds((rows, width), BF16)
    near_bf16 = pltpu.VMEM((rows, width), BF16)

    def forward_local(own):
        return call(
            local_forward, "local_forward", rows, tiles,
            [slab(own_tile, 1, TILE), flat(own_tile), flat(own_tile), whole],
            [
                (held, pltpu.VMEM((tiles, width, rows), BF16)),
                (held, pltpu.VMEM((tiles, width, 2 * HD), F32)),
                (held, pltpu.VMEM((tiles, width, HD), F32)),
                (flat(own_tile), rows_bf16),
                (flat(own_tile), near_bf16),
            ],
            shared, 3 << 30, 16,
        )(first, starts, q, in_hbm(g), own)

    def finish_prev(prev, o, maxes, out, gs):
        out = in_hbm(out)
        return call(
            prev_step, "previous_block", rows, tiles,
            [
                slab(met_tile, 1, TILE), flat(met_tile), flat(met_tile), whole,
                held, held, there, there,
            ],
            [
                (flat(met_tile), rows_bf16), (flat(met_tile), near_bf16),
                (held, pltpu.VMEM((tiles, width, rows), BF16)), (whole, sds((rows, 2 * HD), BF16)),
            ],
            shared + grads, 4 << 30, 16, {7: 0, 8: 1},
        )(first, starts, q, g_near, prev, o, maxes, out, gs)

    def backward_local(gs, out, p, dsp, prev, own):
        out = in_hbm(out)
        return call(
            local_backward, "local_backward", rows, tiles,
            [flat(own_tile), flat(own_tile), flat(own_tile), held, held, whole, whole],
            [(flat(own_tile), rows_bf16), (whole, sds((rows, 2 * HD), F32))],
            grads, 5 << 30, 16,
        )(first, q, gs, out, p, dsp, prev, own)

    return forward_local, finish_prev, backward_local


def pack_kernel(k_ref, v_ref, out_ref):
    for h in range(out_ref.shape[0]):
        out_ref[h, :, :HD] = k_ref[:, h * HD:(h + 1) * HD]
        out_ref[h, :, HD:] = v_ref[:, h * HD:(h + 1) * HD]


def unpack_kernel(x_ref, k_ref, v_ref):
    for h in range(x_ref.shape[0]):
        k_ref[:, h * HD:(h + 1) * HD] = x_ref[h, :, :HD]
        v_ref[:, h * HD:(h + 1) * HD] = x_ref[h, :, HD:]


def pack(keys, values):
    tokens, width = keys.shape
    heads = width // HD
    half = pl.BlockSpec((tokens, width // 2), lambda i: (0, i))
    return pl.pallas_call(
        pack_kernel,
        grid=(2,),
        in_specs=[half, half],
        out_specs=pl.BlockSpec((heads // 2, tokens, 2 * HD), lambda i: (i, 0, 0)),
        out_shape=jax.ShapeDtypeStruct((heads, tokens, 2 * HD), BF16),
        name="pack_heads",
    )(keys, values)


def unpack(x):
    heads, tokens, _ = x.shape
    return pl.pallas_call(
        unpack_kernel,
        in_specs=[pl.BlockSpec(memory_space=pltpu.VMEM)],
        out_shape=[jax.ShapeDtypeStruct((tokens, heads * HD), BF16)] * 2,
        name="unpack_heads",
    )(pltpu.with_memory_space_constraint(x, pltpu.VMEM))


def passed_along(x, axis, by, ring):
    count = lax.axis_size(axis)
    pairs = [(i, (i + by) % count) for i in range(count) if ring or 0 <= i + by < count]
    return lax.ppermute(x, axis, pairs)


def per_device(queries, keys, values, grad_out, doc_lengths):
    rows = queries.shape[0]
    shared = pack(keys, values)
    own = lax.all_to_all(shared, "dp", split_axis=0, concat_axis=0, tiled=True).reshape(rows, 2 * HD)
    first_pos = lax.axis_index("ctx") * rows
    ends = jnp.cumsum(doc_lengths)
    positions = first_pos + jnp.arange(rows, dtype=jnp.int32)
    starts = jnp.max(jnp.where(ends[None, :] <= positions[:, None], ends[None, :], 0), axis=1)
    starts = (starts - first_pos + rows).astype(jnp.int32)
    tiles = rows // TILE
    first = starts[::TILE]
    crossing = jnp.sum(first < rows, dtype=jnp.int32)
    met = jnp.minimum(jnp.arange(tiles, dtype=jnp.int32), jnp.maximum(crossing - 1, 0))
    first = jnp.concatenate([first, met])
    own, first = lax.optimization_barrier((own, first))
    prev = passed_along(own, "ctx", 1, True)
    forward_local, finish_prev, backward_local = attention_calls(
        first, starts.reshape(tiles, 1, TILE), queries, grad_out
    )
    probs, sums, maxes, out, scaled = forward_local(own)
    attn_out, scaled, grad_scores, back = finish_prev(prev, sums, maxes, out, scaled)
    grad_q, mine = backward_local(scaled, attn_out, probs, grad_scores, prev, own)
    total = (mine + passed_along(back, "ctx", -1, False).astype(F32)).astype(BF16)
    total = total.reshape(shared.shape)
    grads = lax.all_to_all(total, "dp", split_axis=0, concat_axis=0, tiled=True)
    grad_k, grad_v = unpack(grads)
    return attn_out, grad_q, grad_k, grad_v


def solution(mesh):
    placed = (P("ctx", "dp"), P(("ctx", "dp"), None), P(("ctx", "dp"), None), P("ctx", "dp"), P())
    return jax.shard_map(
        per_device,
        mesh=mesh,
        in_specs=placed,
        out_specs=(P("ctx", "dp"), P("ctx", "dp"), P(("ctx", "dp"), None), P(("ctx", "dp"), None)),
        check_vma=False,
    )
```

```python
import functools
import math

import jax
import jax.numpy as jnp
from jax import lax
from jax.experimental import pallas as pl
from jax.experimental.pallas import tpu as pltpu
from jax.sharding import PartitionSpec as P

HD = 128
TILE = 128
NEG = -1e30
F32 = jnp.float32
BF16 = jnp.bfloat16
SCALE = 1.0 / math.sqrt(HD)
LOG2_SCALE = SCALE * math.log2(math.e)


def dot_nt(a, b):
    return lax.dot_general(a, b, (((1,), (1,)), ((), ())), preferred_element_type=F32)


def dot_nn(a, b):
    return lax.dot_general(a, b, (((1,), (0,)), ((), ())), preferred_element_type=F32)


def by_rows(ref, heads=None):
    heads = range(ref.shape[1] // HD) if heads is None else heads
    return jnp.concatenate([ref[:, h * HD:(h + 1) * HD] for h in heads], axis=0)


def put_rows(ref, x, heads=None):
    heads = range(ref.shape[1] // HD) if heads is None else heads
    for j, h in enumerate(heads):
        ref[:, h * HD:(h + 1) * HD] = x[j * TILE:(j + 1) * TILE].astype(ref.dtype)


def head_groups(heads, count):
    size = heads // count
    return [(range(j * size, (j + 1) * size), slice(j * size * TILE, (j + 1) * size * TILE)) for j in range(count)]


def write_bias(bias_ref, start_ref, first, count, offset, causal):
    startc = jnp.transpose(jnp.broadcast_to(start_ref[0], (TILE, TILE)))
    lane = lax.broadcasted_iota(jnp.int32, (TILE, TILE), 1)
    row = lax.broadcasted_iota(jnp.int32, (TILE, TILE), 0)
    for j in range(count):
        keep = lane >= startc - ((first + j) * TILE + offset)
        if causal and j == count - 1:
            keep = keep & (lane <= row)
        bias_ref[:, j * TILE:(j + 1) * TILE] = jnp.where(keep, 0.0, NEG)


def biased_scores(q, k, bias, heads):
    t = dot_nt(q, k) * LOG2_SCALE
    rows, width = t.shape
    return (t.reshape(heads, TILE, width) + bias[None]).reshape(rows, width)


def key_tiles(first_ref, i, tiles):
    first = lax.div(first_ref[i], TILE)
    return jnp.minimum(tiles + i - first, i) + 1, jnp.maximum(tiles - first, 0)


def local_forward(first_ref, start_ref, q_ref, g_ref, kv_ref, p_ref, o_ref, max_ref, out_ref, gs_ref, v_s, bias_s):
    i = pl.program_id(0)
    tiles = pl.num_programs(0)
    rows = kv_ref.shape[0]
    heads = q_ref.shape[1] // HD
    here, before = key_tiles(first_ref, i, tiles)

    @pl.when(i == 0)
    def _():
        v_s[:, :HD] = kv_ref[:, HD:]
        v_s[:, HD:] = jnp.ones((rows, HD), BF16)

    for w in range(1, rows // TILE + 1):
        @pl.when(here == w)
        def _(w=w):
            first = i - (w - 1)
            write_bias(bias_s, start_ref, first, w, rows, True)
            keys = pl.ds(pl.multiple_of(first * TILE, TILE), w * TILE)
            for hs, at in head_groups(heads, 2 if w > 3 else 1):
                t = biased_scores(by_rows(q_ref, hs), kv_ref[keys, :HD], bias_s[:, :w * TILE], len(hs))
                m = jnp.max(t, axis=1, keepdims=True)
                p = jnp.exp2(t - m).astype(BF16)
                p_ref[i, at, :w * TILE] = p
                o_ref[i, at] = dot_nn(p, v_s[keys, :])
                max_ref[i, at] = jnp.broadcast_to(m, (m.shape[0], HD))

    @pl.when(before == 0)
    def _():
        finish_rows(o_ref, g_ref, out_ref, gs_ref, i)


def finish_rows(o_ref, g_ref, out_ref, gs_ref, i):
    inv = 1.0 / o_ref[i, :, HD:]
    put_rows(out_ref, o_ref[i, :, :HD] * inv)
    put_rows(gs_ref, by_rows(g_ref).astype(F32) * inv)


def prev_step(first_ref, start_ref, q_ref, g_ref, kv_ref, o_ref, max_ref, out_any, gs_any,
              out_ref, gs_ref, ds_ref, dkv_ref, v_s, bias_s, dk_s, dv_s):
    i = pl.program_id(0)
    rows = kv_ref.shape[0]
    tiles = rows // TILE
    heads = q_ref.shape[1] // HD
    before = key_tiles(first_ref, i, tiles)[1]

    @pl.when(i == 0)
    def _():
        v_s[:, :HD] = kv_ref[:, HD:]
        v_s[:, HD:] = jnp.ones((rows, HD), BF16)
        dk_s[...] = jnp.zeros_like(dk_s)
        dv_s[...] = jnp.zeros_like(dv_s)

    @pl.when((i == 0) & (before == 0))
    def _():
        finish_rows(o_ref, g_ref, out_ref, gs_ref, 0)

    for w in range(1, rows // TILE + 1):
        @pl.when(before == w)
        def _(w=w):
            first = rows // TILE - w
            write_bias(bias_s, start_ref, first, w, 0, False)
            keys = slice(first * TILE, rows)
            for hs, at in head_groups(heads, 1):
                q = by_rows(q_ref, hs)
                g = by_rows(g_ref, hs).astype(F32)
                t = biased_scores(q, kv_ref[keys, :HD], bias_s[:, :w * TILE], len(hs))
                m1 = max_ref[i, at]
                m = jnp.maximum(m1, jnp.max(t, axis=1, keepdims=True))
                a1 = jnp.exp2(m1 - m)
                p = jnp.exp2(t - jnp.concatenate([m] * w, axis=1))
                pb = p.astype(BF16)
                o2 = dot_nn(pb, v_s[keys, :])
                inv = 1.0 / (a1 * o_ref[i, at, HD:] + o2[:, HD:])
                out = ((a1 * o_ref[i, at, :HD] + o2[:, :HD]) * inv).astype(BF16)
                g = g * inv
                gs = g.astype(BF16)
                put_rows(out_ref, out, hs)
                put_rows(gs_ref, g * a1, hs)
                delta = jnp.sum(gs.astype(F32) * out.astype(F32), axis=1, keepdims=True)
                ds = (p * (dot_nt(gs, kv_ref[keys, HD:]) - delta)).astype(BF16)
                ds_ref[i, at, :w * TILE] = ds
                add_grads(dk_s, dv_s, first, w, dot_nn(jnp.transpose(q), ds), dot_nn(jnp.transpose(gs), pb))

    @pl.when(i == pl.num_programs(0) - 1)
    def _():
        write_grads(dkv_ref, dk_s, dv_s, key_tiles(first_ref, 0, tiles)[1])


def add_grads(dk_s, dv_s, first, count, dk, dv):
    for j in range(count):
        dk_s[first + j] += dk[:, j * TILE:(j + 1) * TILE]
        dv_s[first + j] += dv[:, j * TILE:(j + 1) * TILE]


def write_grads(ref, dk_s, dv_s, count):
    tiles = dk_s.shape[0]
    for j in range(tiles):
        at = slice(j * TILE, (j + 1) * TILE)

        @pl.when(j >= tiles - count)
        def _(j=j, at=at):
            ref[at, :HD] = (jnp.transpose(dk_s[j]) * SCALE).astype(ref.dtype)
            ref[at, HD:] = jnp.transpose(dv_s[j]).astype(ref.dtype)

        @pl.when(j < tiles - count)
        def _(at=at):
            ref[at, :] = jnp.zeros((TILE, 2 * HD), ref.dtype)


def local_backward(first_ref, q_ref, gs_ref, out_ref, p_ref, dsp_ref, kvp_ref, kv_ref, dq_ref, dkv_ref, dk_s, dv_s):
    i = pl.program_id(0)
    tiles = pl.num_programs(0)
    rows = kv_ref.shape[0]
    here, before = key_tiles(first_ref, i, tiles)

    @pl.when(i == 0)
    def _():
        dk_s[...] = jnp.zeros_like(dk_s)
        dv_s[...] = jnp.zeros_like(dv_s)

    for w in range(1, rows // TILE + 1):
        @pl.when(here == w)
        def _(w=w):
            first = i - (w - 1)
            keys = pl.ds(pl.multiple_of(first * TILE, TILE), w * TILE)
            for hs, at in head_groups(q_ref.shape[1] // HD, 1):
                q = by_rows(q_ref, hs)
                gs = by_rows(gs_ref, hs)
                pb = p_ref[i, at, :w * TILE]
                delta = jnp.sum(gs.astype(F32) * by_rows(out_ref, hs).astype(F32), axis=1, keepdims=True)
                ds = (pb.astype(F32) * (dot_nt(gs, kv_ref[keys, HD:]) - delta)).astype(BF16)
                put_rows(dq_ref, dot_nn(ds, kv_ref[keys, :HD]) * SCALE, hs)
                add_grads(dk_s, dv_s, first, w, dot_nn(jnp.transpose(q), ds), dot_nn(jnp.transpose(gs), pb))

    for w in range(1, rows // TILE + 1):
        @pl.when(before == w)
        def _(w=w):
            dq = dot_nn(dsp_ref[i, :, :w * TILE], kvp_ref[rows - w * TILE:, :HD]) * SCALE
            put_rows(dq_ref, by_rows(dq_ref).astype(F32) + dq)

    @pl.when(i == tiles - 1)
    def _():
        write_grads(dkv_ref, dk_s, dv_s, tiles)


def call(body, name, rows, steps, ins, outs, scratch, flops, limit, aliases={}):
    big = rows * 4 * HD

    def placed(x):
        if isinstance(x, jax.ShapeDtypeStruct) and math.prod(x.shape) >= big:
            return pltpu.HBM(x.shape, x.dtype)
        return x

    run = pl.pallas_call(
        body,
        grid_spec=pltpu.PrefetchScalarGridSpec(
            num_scalar_prefetch=1, grid=(steps,), in_specs=ins, out_specs=[s for s, _ in outs], scratch_shapes=scratch
        ),
        out_shape=[placed(s) for _, s in outs],
        input_output_aliases=aliases,
        compiler_params=pltpu.CompilerParams(dimension_semantics=("arbitrary",), vmem_limit_bytes=limit << 20),
        cost_estimate=pl.CostEstimate(flops=flops, transcendentals=0, bytes_accessed=8 << 20),
        name=name,
    )
    return run


def in_hbm(x):
    return pltpu.with_memory_space_constraint(x, pltpu.HBM)


def attention_calls(first, starts, q, g):
    rows, width = q.shape
    tiles = rows // TILE
    q = pltpu.with_memory_space_constraint(q, pltpu.VMEM)
    g_near = pltpu.with_memory_space_constraint(g, pltpu.VMEM)
    sds = jax.ShapeDtypeStruct
    own_tile = lambda i, n: i
    met_tile = lambda i, n: n[tiles + i]
    whole = pl.BlockSpec((rows, 2 * HD), lambda i, n: (0, 0))

    def flat(at, w=width):
        return pl.BlockSpec((TILE, w), lambda i, n: (at(i, n), 0))

    def slab(at, *dims):
        return pl.BlockSpec((1,) + dims, lambda i, n: (at(i, n), 0, 0))

    held = pl.BlockSpec(memory_space=pltpu.VMEM)
    there = pl.BlockSpec(memory_space=pl.ANY)
    grads = [pltpu.VMEM((tiles, HD, TILE), F32)] * 2
    shared = [pltpu.VMEM((rows, 2 * HD), BF16), pltpu.VMEM((TILE, rows), F32)]
    rows_bf16 = sds((rows, width), BF16)
    near_bf16 = pltpu.VMEM((rows, width), BF16)

    def forward_local(own):
        return call(
            local_forward, "local_forward", rows, tiles,
            [slab(own_tile, 1, TILE), flat(own_tile), flat(own_tile), whole],
            [
                (held, pltpu.VMEM((tiles, width, rows), BF16)),
                (held, pltpu.VMEM((tiles, width, 2 * HD), F32)),
                (held, pltpu.VMEM((tiles, width, HD), F32)),
                (flat(own_tile), rows_bf16),
                (flat(own_tile), near_bf16),
            ],
            shared, 3 << 30, 16,
        )(first, starts, q, in_hbm(g), own)

    def finish_prev(prev, o, maxes, out, gs):
        out = in_hbm(out)
        return call(
            prev_step, "previous_block", rows, tiles,
            [
                slab(met_tile, 1, TILE), flat(met_tile), flat(met_tile), whole,
                held, held, there, there,
            ],
            [
                (flat(met_tile), rows_bf16), (flat(met_tile), near_bf16),
                (held, pltpu.VMEM((tiles, width, rows), BF16)), (whole, sds((rows, 2 * HD), BF16)),
            ],
            shared + grads, 4 << 30, 16, {7: 0, 8: 1},
        )(first, starts, q, g_near, prev, o, maxes, out, gs)

    def backward_local(gs, out, p, dsp, prev, own):
        out = in_hbm(out)
        return call(
            local_backward, "local_backward", rows, tiles,
            [flat(own_tile), flat(own_tile), flat(own_tile), held, held, whole, whole],
            [(flat(own_tile), rows_bf16), (whole, sds((rows, 2 * HD), F32))],
            grads, 5 << 30, 16,
        )(first, q, gs, out, p, dsp, prev, own)

    return forward_local, finish_prev, backward_local


def pack_kernel(k_ref, v_ref, out_ref):
    for h in range(out_ref.shape[0]):
        out_ref[h, :, :HD] = k_ref[:, h * HD:(h + 1) * HD]
        out_ref[h, :, HD:] = v_ref[:, h * HD:(h + 1) * HD]


def unpack_kernel(x_ref, k_ref, v_ref):
    for h in range(x_ref.shape[0]):
        k_ref[:, h * HD:(h + 1) * HD] = x_ref[h, :, :HD]
        v_ref[:, h * HD:(h + 1) * HD] = x_ref[h, :, HD:]


def pack(keys, values):
    tokens, width = keys.shape
    heads = width // HD
    half = pl.BlockSpec((tokens, width // 2), lambda i: (0, i))
    return pl.pallas_call(
        pack_kernel,
        grid=(2,),
        in_specs=[half, half],
        out_specs=pl.BlockSpec((heads // 2, tokens, 2 * HD), lambda i: (i, 0, 0)),
        out_shape=jax.ShapeDtypeStruct((heads, tokens, 2 * HD), BF16),
        name="pack_heads",
    )(keys, values)


def unpack(x):
    heads, tokens, _ = x.shape
    half = pl.BlockSpec((tokens, heads // 2 * HD), lambda i: (0, i))
    return pl.pallas_call(
        unpack_kernel,
        grid=(2,),
        in_specs=[pl.BlockSpec((heads // 2, tokens, 2 * HD), lambda i: (i, 0, 0))],
        out_specs=[half, half],
        out_shape=[jax.ShapeDtypeStruct((tokens, heads * HD), BF16)] * 2,
        name="unpack_heads",
    )(pltpu.with_memory_space_constraint(x, pltpu.VMEM))


def passed_along(x, axis, by, ring):
    count = lax.axis_size(axis)
    pairs = [(i, (i + by) % count) for i in range(count) if ring or 0 <= i + by < count]
    return lax.ppermute(x, axis, pairs)


def per_device(queries, keys, values, grad_out, doc_lengths):
    rows = queries.shape[0]
    shared = pack(keys, values)
    own = lax.all_to_all(shared, "dp", split_axis=0, concat_axis=0, tiled=True).reshape(rows, 2 * HD)
    first_pos = lax.axis_index("ctx") * rows
    ends = jnp.cumsum(doc_lengths)
    positions = first_pos + jnp.arange(rows, dtype=jnp.int32)
    starts = jnp.max(jnp.where(ends[None, :] <= positions[:, None], ends[None, :], 0), axis=1)
    starts = (starts - first_pos + rows).astype(jnp.int32)
    tiles = rows // TILE
    first = starts[::TILE]
    crossing = jnp.sum(first < rows, dtype=jnp.int32)
    met = jnp.minimum(jnp.arange(tiles, dtype=jnp.int32), jnp.maximum(crossing - 1, 0))
    first = jnp.concatenate([first, met])
    own, first = lax.optimization_barrier((own, first))
    prev = passed_along(own, "ctx", 1, True)
    forward_local, finish_prev, backward_local = attention_calls(
        first, starts.reshape(tiles, 1, TILE), queries, grad_out
    )
    probs, sums, maxes, out, scaled = forward_local(own)
    attn_out, scaled, grad_scores, back = finish_prev(prev, sums, maxes, out, scaled)
    grad_q, mine = backward_local(scaled, attn_out, probs, grad_scores, prev, own)
    total = (mine + passed_along(back, "ctx", -1, False).astype(F32)).astype(BF16)
    total = total.reshape(shared.shape)
    grads = lax.all_to_all(total, "dp", split_axis=0, concat_axis=0, tiled=True)
    grad_k, grad_v = unpack(grads)
    return attn_out, grad_q, grad_k, grad_v


def solution(mesh):
    placed = (P("ctx", "dp"), P(("ctx", "dp"), None), P(("ctx", "dp"), None), P("ctx", "dp"), P())
    return jax.shard_map(
        per_device,
        mesh=mesh,
        in_specs=placed,
        out_specs=(P("ctx", "dp"), P("ctx", "dp"), P(("ctx", "dp"), None), P(("ctx", "dp"), None)),
        check_vma=False,
    )
```
